32 devices in a mesh: groups: 2 (over x), section: 1, expert: 16 (over z, y, core).
Axes of the slice: x: 2, y: 2, z: 4, core: 2. Of those that a mesh axis runs over, the one named last changes fastest.
Arguments:
- inputs: bfloat16 [2, 512, 2048], P(None, ('groups', 'expert')), parts along dimension 1, may hold values from -6 to 6
- routes: int32 [2, 2, 512, 8], P('section', None, ('groups', 'expert')), parts along dimension 2, may hold values from 0 to 15, all different within a row; in each aligned block of 16 rows (0 to 15, 16 to 31, ..., all dimensions but the last counted through in order) at most 16 rows name the same one
- norm_gain: float32 [2, 2048], P('section'), may hold values from 0.1 to 1.9
- w_gate_up: bfloat16 [2, 16, 2048, 1536], P('section', 'expert'), may hold values from -0.125 to 0.125
- w_down: bfloat16 [2, 16, 768, 2048], P('section', 'expert'), may hold values from -0.4375 to 0.4375
Outputs:
- outputs: bfloat16 [2, 2, 512, 2048], P('section', None, ('groups', 'expert')), parts along dimension 2
The draws below stay inside these ranges and needn't reach their ends.
There are 2 independent parts, one for each index of `groups`. The reference program is written for one: setup_inputs(seed, part) draws one part's arguments, and reference() takes and returns one part's arrays. A program takes and returns all parts, laid end to end along the dimension named above; an argument that names none is the same for every part. Nothing has to cross between parts.
Inputs may be any that keep to these rules, and one draw needn't show every extreme that they name: `routes`: the 8 entries of a row differ. In each aligned block of 16 rows (the rows of one index of expert in one micro-batch of one layer) no expert is named by more than 16 rows, and some block reaches 16.
All inputs are finite; a program needn't handle non-finite values.
Results may differ from the reference program's by a relative error of at most 0.0055.
Values may be sent and summed in bfloat16 or wider, within the bound.
A program may use at most 64 MiB of HBM per device.

```python
import math
import jax
import jax.numpy as jnp
import numpy as np
from jax import lax

D = 2048
F = 768
TOP = 8
MB = 2
TOK_MB = 16
EXPERTS = 16
TOKENS = 256
CAP = 16


def block_levels(own_key, extent, cuts, least, largest):
    level = 1.0
    for position, shards_of in cuts:
        steps = jax.random.uniform(jax.random.fold_in(jax.random.fold_in(own_key, 6), position), (shards_of,), jnp.float32, least / len(cuts), largest / len(cuts))
        level = level * jnp.repeat(jnp.exp(steps), extent[position] // shards_of).reshape((-1,) + (1,) * (len(extent) - 1 - position))
    return level


def deal_out(stream_key, own, number, rows, number_of, top, most, skew):
    order = jax.random.permutation(stream_key, number_of)
    crowded, usual = load_shares(number_of, rows * top, most, skew, True), load_shares(number_of, rows * top, most, skew, False)
    places = jnp.arange(number_of)

    def named(tallies, rotation):
        used = int((tallies > 0).sum())
        fixed = max(1, used // 4)
        moved = fixed + (places - fixed + rotation * (used - fixed)) % max(1, number_of - fixed)
        return jnp.zeros((number_of,), jnp.int32).at[order[jnp.where(places < fixed, places, moved)]].set(jnp.asarray(tallies, jnp.int32))

    tallies = jnp.where(number % 4 == 0, named(crowded, number // 4), named(usual, number - number // 4 - 1))
    mixed = jax.random.permutation(jax.random.fold_in(own, 3), number_of)
    giver, sink = mixed[0:number_of // 2 * 2:2], mixed[1:number_of // 2 * 2:2]
    slack = jnp.minimum(tallies[giver] - 1, most - tallies[sink]) // 2
    slack = jnp.where((giver == order[0]) | (sink == order[0]) | (tallies[sink] == 0), 0, jnp.maximum(slack, 0))
    moved = jax.random.randint(jax.random.fold_in(own, 4), (number_of // 2,), 0, 1 << 20) % (slack + 1)
    tallies = tallies.at[giver].add(-moved).at[sink].add(moved)
    items = jnp.searchsorted(jnp.cumsum(tallies), jnp.arange(rows * top), side="right").astype(jnp.int32)
    listing = items.reshape(top, rows).T
    listing = listing[jax.random.permutation(jax.random.fold_in(own, 1), rows)]
    rotation = jax.random.randint(jax.random.fold_in(own, 2), (rows, 1), 0, top)
    return jnp.take_along_axis(listing, (jnp.arange(top)[None, :] + rotation) % top, axis=1)


def load_shares(amount, total, most, skew, full):
    weights = [(1 << 20) // math.isqrt(grade ** skew) + 1 for grade in range(1, amount + 1)]
    largest = most if full else min(most, max(-(-total // amount), total * weights[0] // sum(weights)))
    least = 1 if total - largest >= amount - 1 else 0
    given, spare = [largest] + [least] * (amount - 1), total - largest - least * (amount - 1)
    while spare > 0:
        candidates = [i for i in range(1, amount) if given[i] < largest] or [i for i in range(1, amount) if given[i] < most]
        pool, budget = sum([weights[i] for i in candidates]), spare
        for i in candidates:
            addition = min(most - given[i], max(1, budget * weights[i] // pool), spare)
            given[i] = given[i] + addition
            spare = spare - addition
    return np.array(given)


def gaussian(stream_key, extent, deviation, bound, split=(), held_as=jnp.bfloat16):
    level = block_levels(stream_key, extent, split, -0.22, 0.18) if split else 1.0
    drawn = jax.random.normal(stream_key, extent, jnp.float32) * deviation * level
    return jnp.minimum(jnp.maximum(drawn, -bound), bound).astype(held_as)


def setup_inputs(seed: int = 0, part: int = 0) -> dict:
    splits = jax.random.split(jax.random.key(seed), 6)
    part_splits = jax.random.split(jax.random.fold_in(splits[5], part), 6)
    inputs = gaussian(part_splits[0], (MB, TOKENS, D), 1.0, 6.0, ((1, 16),))
    routes_keys = jax.random.split(jax.random.fold_in(part_splits[1], 1), 2 * MB * TOKENS // TOK_MB)
    routes_turns = jax.random.permutation(jax.random.fold_in(part_splits[1], 3), 2 * MB * TOKENS // TOK_MB)
    routes = jax.vmap(lambda own, number: deal_out(jax.random.fold_in(part_splits[1], 2), own, number, TOK_MB, EXPERTS, TOP, CAP, 2))(routes_keys, routes_turns).reshape((2, MB, TOKENS, TOP))
    norm_gain = jnp.clip(1.0 + 0.18 * jax.random.normal(splits[2], (2, D), jnp.float32), 0.1, 1.9)
    w_gate_up = gaussian(splits[3], (2, EXPERTS, D, 2 * F), D ** -0.5, 0.125, ((1, 16),))
    w_down = gaussian(splits[4], (2, EXPERTS, F, D), (F // 4) ** -0.5, 0.4375, ((1, 16),))
    return dict(inputs=inputs, routes=routes, norm_gain=norm_gain, w_gate_up=w_gate_up, w_down=w_down)


eps = 1e-06

def expert_ffn(rows, gate_up, down_proj):
    joined = jnp.dot(rows.astype(jnp.float32), gate_up.astype(jnp.float32))
    hidden = (jax.nn.silu(joined[:, :F]) * joined[:, F:]).astype(jnp.bfloat16)
    return jnp.dot(hidden.astype(jnp.float32), down_proj.astype(jnp.float32)).astype(jnp.bfloat16)

def moe_layer(current, layer_routes, gain_row, gate_up, down_proj):
    widened = current.astype(jnp.float32)
    scale_inv = lax.rsqrt(lax.optimization_barrier(jnp.mean(widened * widened, axis=-1, keepdims=True)) + eps)
    normed = (widened * scale_inv * gain_row).astype(jnp.bfloat16)
    flat_routes = layer_routes.reshape(-1).astype(jnp.int32)
    expert_ids = jnp.arange(EXPERTS, dtype=jnp.int32)
    onehot = (flat_routes[:, None] == expert_ids[None, :]).astype(jnp.int32)
    before = jnp.cumsum(onehot, axis=0) - onehot
    rank_of = lax.optimization_barrier(jnp.sum(before * onehot, axis=1))
    room = EXPERTS * CAP
    target = (flat_routes * room + rank_of).astype(jnp.int32)
    source = jnp.repeat(normed, TOP, axis=0)
    buffer = jnp.zeros((EXPERTS * room, D), jnp.bfloat16).at[target].set(source)
    results = lax.map(lambda packed: expert_ffn(packed[0], packed[1], packed[2]), (buffer.reshape(EXPERTS, room, D), gate_up, down_proj))
    picked = results.reshape(EXPERTS * room, D)[target].reshape(TOKENS, TOP, D).astype(jnp.float32)
    combined = lax.optimization_barrier(jnp.sum(picked, axis=1)) * 0.125
    return (widened + combined).astype(jnp.bfloat16)

def reference(inputs, routes, norm_gain, w_gate_up, w_down):
    first_layer = []
    for batch_no in range(MB):
        first_layer.append(moe_layer(inputs[batch_no], routes[0, batch_no], norm_gain[0], w_gate_up[0], w_down[0]))
    second_layer = []
    for batch_no in range(MB):
        second_layer.append(moe_layer(first_layer[batch_no], routes[1, batch_no], norm_gain[1], w_gate_up[1], w_down[1]))
    return jnp.stack([jnp.stack(first_layer), jnp.stack(second_layer)])
```

```python
import functools

import jax
import jax.numpy as jnp
from jax import lax
from jax.experimental import pallas as pl
from jax.experimental.pallas import tpu as pltpu
from jax.sharding import PartitionSpec as P

eps = 1e-06


def from_behind(value, axis, steps):
    count = lax.axis_size(axis)
    initial, last = (max(0, -steps), min(count, count - steps))
    return lax.ppermute(value, axis, [(source, source + steps) for source in range(initial, last)])


def expert_rows(rows, gate_up, down_proj):
    hidden_size = down_proj.shape[0]
    joined = jnp.dot(rows, gate_up, preferred_element_type=jnp.float32)
    hidden = (jax.nn.silu(joined[:, :hidden_size]) * joined[:, hidden_size:]).astype(jnp.bfloat16)
    return jnp.dot(hidden, down_proj, preferred_element_type=jnp.float32).astype(jnp.bfloat16)


def run_experts(received, gate_up, down_proj):
    flat = received.reshape(-1, received.shape[2])
    done = expert_rows(flat, gate_up, down_proj)
    return done.reshape(received.shape)


def moe_layer(current, layer_routes, gain_row, gate_up, down_proj, experts, capacity):
    tokens, features = current.shape
    widened = current.astype(jnp.float32)
    scale_inv = lax.rsqrt(jnp.mean(widened * widened, axis=-1, keepdims=True) + eps)
    normed = (widened * scale_inv * gain_row).astype(jnp.bfloat16)
    expert_ids = jnp.arange(experts, dtype=jnp.int32)
    onehot = (layer_routes[:, :, None] == expert_ids[None, None, :]).astype(jnp.int32)
    counted = jnp.sum(onehot, axis=1)
    before = jnp.cumsum(counted, axis=0) - counted
    slot_of = jnp.sum(onehot * (expert_ids[None, None, :] * capacity + before[:, None, :]), axis=2)
    slot_ids = jnp.arange(experts * capacity, dtype=jnp.int32)
    placing = jnp.sum(
        (slot_ids[:, None, None] == slot_of[None, :, :]).astype(jnp.int32), axis=2
    ).astype(jnp.bfloat16)
    outgoing = jnp.dot(placing, normed, preferred_element_type=jnp.float32).astype(jnp.bfloat16)
    outgoing = outgoing.reshape(experts, capacity, features)
    results = run_experts(
        lax.all_to_all(outgoing, "expert", split_axis=0, concat_axis=0, tiled=True),
        gate_up,
        down_proj,
    )
    returned = lax.all_to_all(results, "expert", split_axis=0, concat_axis=0, tiled=True).reshape(
        experts * capacity, features
    )
    combined = (
        jnp.einsum("it,id->td", placing, returned, preferred_element_type=jnp.float32) * 0.125
    )
    return (widened + combined).astype(jnp.bfloat16)


def on_device(inputs, routes, norm_gain, w_gate_up, w_down):
    experts = lax.axis_size("expert")
    sections = lax.axis_size("section")
    batches, tokens, features = inputs.shape
    top_k = routes.shape[3]
    capacity = min(tokens, 2 * tokens * top_k // experts)
    if sections == 1:
        layers_out = []
        previous = [inputs[batch_no] for batch_no in range(batches)]
        for layer_no in range(routes.shape[0]):
            current_layer = []
            for batch_no in range(batches):
                current_layer.append(
                    moe_layer(
                        previous[batch_no],
                        routes[layer_no, batch_no],
                        norm_gain[layer_no],
                        w_gate_up[layer_no, 0],
                        w_down[layer_no, 0],
                        experts,
                        capacity,
                    )
                )
            layers_out.append(jnp.stack(current_layer))
            previous = current_layer
        return jnp.stack(layers_out)
    segment_no = lax.axis_index("section")
    layer_routes = routes[0]
    gain_row = norm_gain[0]
    gate_up = w_gate_up[0, 0]
    down_proj = w_down[0, 0]
    handed = jnp.zeros((tokens, features), jnp.bfloat16)
    finished = []
    for turn_no in range(batches + 1):
        if turn_no < batches:
            fresh_rows = inputs[turn_no]
        else:
            fresh_rows = jnp.zeros((tokens, features), jnp.bfloat16)
        current = jnp.where(segment_no == 0, fresh_rows, handed)
        batch_pick = jnp.clip(turn_no - segment_no, 0, batches - 1)
        turn_routes = lax.dynamic_index_in_dim(layer_routes, batch_pick, 0, keepdims=False)
        result = moe_layer(current, turn_routes, gain_row, gate_up, down_proj, experts, capacity)
        finished.append(result)
        if turn_no < batches:
            handed = from_behind(result, "section", 1)
    first_segment = jnp.stack(finished[:batches])
    second_segment = jnp.stack(finished[1:])
    return jnp.where(segment_no == 0, first_segment, second_segment)[None]

LANES = 128
PAIR = 2
DEPTH = 4
TILE = 256
CHUNKS = 2
DOWN_PARTS = 2
KINDS = ("own", "z_in", "y_in", "y_out", "z_out", "done", "up", "down")
END_ORDER = (
    0, 4, 8, 45, 33, 12, 37, 34, 77, 46, 35, 65, 38, 39, 64, 41,
    66, 69, 72, 67, 43, 192, 70, 68, 42, 71, 47, 193, 194, 73, 196, 75,
    197, 198, 224, 74, 225, 76, 78, 79, 228, 229, 200, 99, 98, 201, 202, 97,
    204, 205, 102, 103, 101, 206, 96, 232, 131, 233, 130, 236, 107, 106, 129, 237,
    105, 134, 135, 133, 108, 110, 139, 160, 111, 100, 109, 16, 138, 142, 143, 164,
    104, 20, 49, 137, 141, 168, 51, 24, 80, 53, 50, 84, 83, 54, 172, 55,
    28, 82, 57, 81, 86, 85, 61, 87, 208, 59, 209, 210, 58, 212, 89, 213,
    62, 214, 240, 91, 63, 241, 92, 244, 88, 90, 245, 94, 93, 113, 114, 216,
    95, 217, 118, 218, 117, 115, 220, 221, 119, 222, 248, 145, 249, 116, 146, 252,
    150, 253, 123, 122, 127, 126, 147, 151, 155, 121, 124, 125, 154, 159, 158, 153,
    149, 120, 157, 112, 180, 176, 188, 184,
)
INNER_ORDER = (
    0, 12, 4, 8, 33, 34, 76, 45, 35, 38, 37, 68, 39, 43, 41, 67,
    64, 66, 72, 65, 192, 47, 69, 193, 42, 194, 71, 46, 77, 70, 196, 197,
    79, 198, 73, 74, 224, 75, 78, 225, 228, 229, 200, 201, 96, 98, 101, 202,
    97, 204, 205, 102, 206, 232, 99, 233, 130, 236, 103, 237, 134, 106, 104, 107,
    131, 129, 111, 100, 109, 105, 138, 133, 135, 110, 139, 160, 164, 108, 50, 16,
    20, 51, 137, 142, 49, 53, 141, 82, 143, 54, 55, 168, 83, 24, 80, 172,
    28, 85, 84, 81, 59, 208, 87, 86, 57, 209, 61, 210, 212, 213, 62, 58,
    88, 91, 63, 214, 240, 241, 244, 245, 118, 113, 89, 93, 92, 90, 94, 95,
    216, 217, 218, 117, 119, 220, 112, 114, 221, 222, 248, 249, 115, 121, 252, 253,
    150, 122, 120, 146, 123, 116, 145, 126, 127, 125, 154, 149, 147, 151, 155, 124,
    176, 153, 158, 159, 157, 184, 180, 188,
)


def flat_rows(block):
    return block.reshape(-1, block.shape[-1])


def unpack(code):
    code, number = divmod(code, 4)
    code, chunk = divmod(code, CHUNKS)
    code, batch = divmod(code, 2)
    kind, layer = divmod(code, 2)
    return KINDS[kind], layer, batch, chunk, number


def moe_kernel(
    count,
    x_hbm,
    routes_hbm,
    gain_hbm,
    gu_hbm,
    down_hbm,
    out_ref,
    x_ref,
    routes_ref,
    gain_ref,
    gu,
    down,
    rows,
    scaled,
    squares,
    joined,
    hidden,
    made,
    from_core,
    to_y,
    from_y,
    to_z,
    from_z,
    passing,
    x_sem,
    w_sem,
    az_s,
    az_r,
    ap_s,
    ay_s,
    ay_r,
    ac_s,
    ac_r,
    rc_s,
    rc_r,
    ry_s,
    ry_r,
    rz_s,
    rz_r,
    rp_r,
):
    layers, batches = routes_ref.shape[0], routes_ref.shape[1]
    tokens, features = x_ref.shape[1], x_ref.shape[2]
    units = down.shape[1]
    width = features // CHUNKS
    me = lax.axis_index("expert")
    c = lax.rem(me, PAIR)
    y = lax.rem(lax.div(me, PAIR), PAIR)
    z = lax.div(me, PAIR * PAIR)
    other_c, other_y = 1 - c, 1 - y

    def expert_at(zz, yy, cc):
        return (zz * PAIR + yy) * PAIR + cc

    low = z < DEPTH // 2
    inner = jnp.logical_and(z > 0, z < DEPTH - 1)

    def ranked(at_end, at_inner):
        upward = jnp.where(inner, at_inner, at_end)
        return jnp.where(low, upward, DEPTH - 1 - upward)

    near = [z, ranked(1, 2), ranked(2, 0), ranked(3, 3)]
    core_peer = expert_at(z, y, other_c)
    y_peer = expert_at(z, other_y, c)
    z_peers = [me] + [expert_at(near[n], y, c) for n in range(1, DEPTH)]

    def remote(src, dst, send, recv, target):
        return pltpu.make_async_remote_copy(
            src_ref=src,
            dst_ref=dst,
            send_sem=send,
            recv_sem=recv,
            device_id={"expert": target},
            device_id_type=pl.DeviceIdType.MESH,
        )

    barrier = pltpu.get_barrier_semaphore()
    for peer in z_peers[1:] + [core_peer, y_peer]:
        pl.semaphore_signal(
            barrier, inc=1, device_id={"expert": peer}, device_id_type=pl.DeviceIdType.MESH
        )

    inputs = ((x_hbm, x_ref), (routes_hbm, routes_ref), (gain_hbm, gain_ref))
    small = [
        pltpu.make_async_copy(source, target, x_sem.at[number])
        for number, (source, target) in enumerate(inputs)
    ]
    for load in small:
        load.start()
    for load in small:
        load.wait()
    loads = []
    for layer in range(layers):
        for number, (source, target) in enumerate(((gu_hbm, gu), (down_hbm, down))):
            load = pltpu.make_async_copy(
                source.at[layer, 0], target.at[layer], w_sem.at[layer, number]
            )
            load.start()
            loads.append(load)

    lanes = lax.broadcasted_iota(jnp.int32, (LANES, tokens), 0)
    named = jnp.zeros((LANES, tokens), jnp.float32)
    for lay in range(layers):
        for bat in range(batches):
            chosen = routes_ref[lay, bat] + (lay * batches + bat) * count
            for k in range(chosen.shape[0]):
                named = named + (chosen[k : k + 1, :] == lanes).astype(jnp.float32)
    same = lax.broadcasted_iota(jnp.int32, (tokens, tokens), 0) == lax.broadcasted_iota(
        jnp.int32, (tokens, tokens), 1
    )
    named = lax.dot_general(
        same.astype(jnp.bfloat16),
        named.astype(jnp.bfloat16),
        (((1,), (1,)), ((), ())),
        preferred_element_type=jnp.float32,
    )
    rows[0, c, y, z, :, pl.ds(features, LANES)] = named.astype(jnp.bfloat16)
    for bat in range(batches):
        rows[bat, c, y, z, :, pl.ds(0, features)] = x_ref[bat]
    pl.semaphore_wait(barrier, DEPTH + 1)

    def slot(layer, batch):
        return layer * batches + batch

    def cols(h):
        return pl.ds(h * width, width)

    def row_block(s, h, cc, yy, zz):
        extra = LANES if s == 0 and h == CHUNKS - 1 else 0
        return rows.at[s, cc, yy, zz, :, pl.ds(h * width, width + extra)]

    def gather_core(s, h, cc, yy, zz):
        block = row_block(s, h, cc, yy, zz)
        return remote(block, block, ac_s.at[s, h, yy, zz], ac_r.at[s, h, yy, zz], core_peer)

    def gather_y(s, h, yy, zz):
        block = row_block(s, h, c, yy, zz)
        return remote(block, block, ay_s.at[s, h, zz], ay_r.at[s, h, zz], y_peer)

    def gather_z(s, h, n):
        block = row_block(s, h, c, y, z)
        return remote(block, block, az_s.at[s, h, n], az_r.at[s, h, z], z_peers[n])

    def gather_z_from(s, h, n):
        block = row_block(s, h, c, y, near[n])
        return remote(block, block, ap_s.at[s, h, n], az_r.at[s, h, near[n]], z_peers[2])

    def sum_core(s, h, cc, yy):
        return remote(
            made.at[s, cc, yy, :, :, cols(h)],
            from_core.at[s, yy, :, :, cols(h)],
            rc_s.at[s, h, yy],
            rc_r.at[s, h, yy],
            core_peer,
        )

    def sum_y(s, h, zz):
        return remote(
            to_y.at[s, zz, :, cols(h)],
            from_y.at[s, zz, :, cols(h)],
            ry_s.at[s, h, zz],
            ry_r.at[s, h, zz],
            y_peer,
        )

    def sum_z(s, h, n, source):
        return remote(
            to_z.at[s, near[n], :, cols(h)],
            from_z.at[s, source, :, cols(h)],
            rz_s.at[s, h, n],
            rz_r.at[s, h, source],
            z_peers[n],
        )

    def sum_pass(s, h, n):
        return remote(
            to_z.at[s, near[n], :, cols(h)],
            passing.at[s, near[n], :, cols(h)],
            rz_s.at[s, h, n],
            rp_r.at[s, h, near[n]],
            z_peers[1],
        )

    def pair_sum(s, h, yy, zz):
        return made[s, c, yy, zz, :, cols(h)].astype(jnp.float32) + from_core[
            s, yy, zz, :, cols(h)
        ].astype(jnp.float32)

    class Place:
        def __init__(self, at_end):
            self.at_end = at_end
            self.sends = []
            self.seen = set()

        def go(self, build, *args):
            build(*args).start()
            self.sends.append((build, args))

        def once(self, build, *args, key):
            if (build, key) not in self.seen:
                self.seen.add((build, key))
                build(*args).wait_recv()

        def own(self, layer, batch, h, n):
            s = slot(layer, batch)
            self.go(gather_y, s, h, y, z)
            self.go(gather_z, s, h, 1)
            self.go(gather_z, s, h, 2)
            self.go(gather_core, s, h, c, y, z)

        def z_in(self, layer, batch, h, n):
            s = slot(layer, batch)
            gather_z_from(s, h, n).wait_recv()
            if not self.at_end and n != 2:
                self.go(gather_z_from, s, h, n)
            self.go(gather_y, s, h, y, near[n])
            self.go(gather_core, s, h, c, y, near[n])

        def y_in(self, layer, batch, h, n):
            s = slot(layer, batch)
            gather_y(s, h, other_y, near[n]).wait_recv()
            self.go(gather_core, s, h, c, other_y, near[n])

        def y_out(self, layer, batch, h, n):
            s = slot(layer, batch)
            self.once(sum_core, s, h, other_c, other_y, key=(s, h, 1))
            to_y[s, near[n], :, cols(h)] = pair_sum(s, h, other_y, near[n]).astype(jnp.bfloat16)
            self.go(sum_y, s, h, near[n])

        def z_out(self, layer, batch, h, n):
            s = slot(layer, batch)
            zz = near[n]
            self.once(sum_core, s, h, other_c, y, key=(s, h, 0))
            sum_y(s, h, zz).wait_recv()
            total = pair_sum(s, h, y, zz) + from_y[s, zz, :, cols(h)].astype(jnp.float32)
            if not self.at_end and n != 2:
                sum_pass(s, h, n).wait_recv()
                total = total + passing[s, zz, :, cols(h)].astype(jnp.float32)
            to_z[s, zz, :, cols(h)] = total.astype(jnp.bfloat16)
            if self.at_end and n != 1:
                self.go(sum_pass, s, h, n)
            else:
                self.go(sum_z, s, h, n, z)

        def done(self, layer, batch, h, n):
            s = slot(layer, batch)
            self.once(sum_core, s, h, other_c, y, key=(s, h, 0))
            sum_y(s, h, z).wait_recv()
            total = pair_sum(s, h, y, z) + from_y[s, z, :, cols(h)].astype(jnp.float32)
            for r in (1, 2):
                sum_z(s, h, r, near[r]).wait_recv()
                total = total + from_z[s, near[r], :, cols(h)].astype(jnp.float32)
            source = x_ref if layer == 0 else out_ref.at[layer - 1]
            value = source[batch, :, cols(h)].astype(jnp.float32) + total * 0.125
            value = value.astype(jnp.bfloat16)
            out_ref[layer, batch, :, cols(h)] = value
            if layer + 1 < layers:
                rows[slot(layer + 1, batch), c, y, z, :, cols(h)] = value

        def drain(self):
            for build, args in self.sends:
                build(*args).wait_send()

    end, inside = Place(True), Place(False)

    def up(layer, batch, k, u):
        s = slot(layer, batch)
        if u == 0:
            for yy in (y, other_y):
                for n in range(DEPTH):
                    gather_core(s, k, other_c, yy, near[n]).wait_recv()
            if k == 0 and batch == 0:
                loads[2 * layer].wait()
            h = flat_rows(rows[s, :, :, :, :, cols(k)]).astype(jnp.float32)
            part = jnp.sum(h * h, axis=-1, keepdims=True)
            squares[...] = part if k == 0 else squares[...] + part
            scaled[...] = (h * gain_ref[pl.ds(layer, 1), cols(k)]).astype(jnp.bfloat16)
        x = scaled[...]
        mine_cols = (pl.ds(u * TILE, TILE), pl.ds(units + u * TILE, TILE))
        gate, lift = (
            jnp.dot(x, gu[layer, cols(k), where], preferred_element_type=jnp.float32)
            for where in mine_cols
        )
        if k > 0:
            gate, lift = joined[:, mine_cols[0]] + gate, joined[:, mine_cols[1]] + lift
        if k < CHUNKS - 1:
            joined[:, mine_cols[0]] = gate
            joined[:, mine_cols[1]] = lift
            return
        named = flat_rows(rows[0, :, :, :, :, pl.ds(features, LANES)]).astype(jnp.float32)
        lanes = lax.broadcasted_iota(jnp.int32, named.shape, 1)
        mine = jnp.sum(jnp.where(lanes == me + s * count, named, 0.0), axis=1, keepdims=True) > 0.5
        scale = lax.rsqrt(squares[...] * (1.0 / features) + eps)
        gate, lift = gate * scale, lift * scale
        value = gate / (1.0 + jnp.exp(-gate)) * lift
        hidden[:, pl.ds(u * TILE, TILE)] = jnp.where(mine, value, 0.0).astype(jnp.bfloat16)

    def down_part(layer, batch, h, u):
        s = slot(layer, batch)
        if h == 0 and u == 0 and batch == 0:
            loads[2 * layer + 1].wait()
        parts = DOWN_PARTS
        size = width // parts

        for j in range(size // TILE):
            where = pl.ds(h * width + u * size + j * TILE, TILE)
            result = jnp.dot(hidden[...], down[layer, :, where], preferred_element_type=jnp.float32)
            made[s, :, :, :, :, where] = result.astype(jnp.bfloat16).reshape(
                PAIR, PAIR, DEPTH, tokens, TILE
            )
        if u == parts - 1:
            for place, guard in ((end, jnp.logical_not(inner)), (inside, inner)):
                place.sends.append((sum_core, (s, h, other_c, other_y)))
                place.sends.append((sum_core, (s, h, other_c, y)))
            sum_core(s, h, other_c, other_y).start()
            sum_core(s, h, other_c, y).start()

    def steps(place, codes):
        for code in codes:
            kind, *rest = unpack(code)
            getattr(place, kind)(*rest)

    def both(codes_end, codes_inside):
        if codes_end:
            pl.when(jnp.logical_not(inner))(functools.partial(steps, end, codes_end))
        if codes_inside:
            pl.when(inner)(functools.partial(steps, inside, codes_inside))

    def split(order):
        parts, heads = [[]], []
        for code in order:
            if unpack(code)[0] in ("up", "down"):
                heads.append(code)
                parts.append([])
            else:
                parts[-1].append(code)
        return parts, heads

    parts_end, heads = split(END_ORDER)
    parts_inside, _ = split(INNER_ORDER)
    both(parts_end[0], parts_inside[0])
    for code, codes_end, codes_inside in zip(heads, parts_end[1:], parts_inside[1:]):
        kind, *rest = unpack(code)
        (up if kind == "up" else down_part)(*rest)
        both(codes_end, codes_inside)
    pl.when(jnp.logical_not(inner))(end.drain)
    pl.when(inner)(inside.drain)


def fused_on_device(count, inputs, routes, norm_gain, w_gate_up, w_down):
    batches, tokens, features = inputs.shape
    layers = routes.shape[0]
    units = w_down.shape[2]
    slots = layers * batches
    bf16 = jnp.bfloat16
    vmem = pl.BlockSpec(memory_space=pltpu.VMEM)
    hbm = pl.BlockSpec(memory_space=pl.ANY)
    dma = pltpu.SemaphoreType.DMA
    by_z = pltpu.VMEM((slots, DEPTH, tokens, features), bf16)
    every = dma((slots, CHUNKS, DEPTH))
    return pl.pallas_call(
        functools.partial(moe_kernel, count),
        out_shape=jax.ShapeDtypeStruct((layers, batches, tokens, features), bf16),
        in_specs=[hbm] * 5,
        out_specs=vmem,
        scratch_shapes=[
            pltpu.VMEM((batches, tokens, features), bf16),
            pltpu.VMEM((layers, batches, routes.shape[3], tokens), jnp.int32),
            pltpu.VMEM((layers, features), jnp.float32),
            pltpu.VMEM((layers, features, 2 * units), bf16),
            pltpu.VMEM((layers, units, features), bf16),
            pltpu.VMEM((slots, PAIR, PAIR, DEPTH, tokens, features + LANES), bf16),
            pltpu.VMEM((count * tokens, features // CHUNKS), bf16),
            pltpu.VMEM((count * tokens, 1), jnp.float32),
            pltpu.VMEM((count * tokens, 2 * units), jnp.float32),
            pltpu.VMEM((count * tokens, units), bf16),
            pltpu.VMEM((slots, PAIR, PAIR, DEPTH, tokens, features), bf16),
            pltpu.VMEM((slots, PAIR, DEPTH, tokens, features), bf16),
            by_z,
            by_z,
            by_z,
            by_z,
            by_z,
            dma((3,)),
            dma((layers, 2)),
            every,
            every,
            every,
            every,
            every,
            dma((slots, CHUNKS, PAIR, DEPTH)),
            dma((slots, CHUNKS, PAIR, DEPTH)),
            dma((slots, CHUNKS, PAIR)),
            dma((slots, CHUNKS, PAIR)),
            every,
            every,
            every,
            every,
            every,
        ],
        compiler_params=pltpu.CompilerParams(
            collective_id=0, has_side_effects=True, vmem_limit_bytes=60 << 20
        ),
        name="moe",
    )(inputs, jnp.swapaxes(routes, 2, 3), norm_gain, w_gate_up, w_down)


def choose(count, inputs, routes, norm_gain, w_gate_up, w_down):
    batches, tokens, features = inputs.shape
    layers = routes.shape[0]
    fits = layers == 2 and batches == 2 and layers * batches * count <= LANES
    tiled = w_down.shape[2] == 3 * TILE and features % (CHUNKS * DOWN_PARTS * TILE) == 0
    run = functools.partial(fused_on_device, count) if fits and tiled and tokens % 16 == 0 else on_device
    return run(inputs, routes, norm_gain, w_gate_up, w_down)


def solution(mesh):
    placed = (
        P(None, ("groups", "expert"), None),
        P("section", None, ("groups", "expert"), None),
        P("section", None),
        P("section", "expert", None, None),
        P("section", "expert", None, None),
    )
    count = mesh.shape["expert"]
    fused = mesh.shape["section"] == 1 and count == PAIR * PAIR * DEPTH
    return jax.shard_map(
        functools.partial(choose, count) if fused else on_device,
        mesh=mesh,
        in_specs=placed,
        out_specs=P("section", None, ("groups", "expert"), None),
        check_vma=False,
    )
```

```python
import functools

import jax
import jax.numpy as jnp
from jax import lax
from jax.experimental import pallas as pl
from jax.experimental.pallas import tpu as pltpu
from jax.sharding import PartitionSpec as P

eps = 1e-06


def from_behind(value, axis, steps):
    count = lax.axis_size(axis)
    initial, last = (max(0, -steps), min(count, count - steps))
    return lax.ppermute(value, axis, [(source, source + steps) for source in range(initial, last)])


def expert_rows(rows, gate_up, down_proj):
    hidden_size = down_proj.shape[0]
    joined = jnp.dot(rows, gate_up, preferred_element_type=jnp.float32)
    hidden = (jax.nn.silu(joined[:, :hidden_size]) * joined[:, hidden_size:]).astype(jnp.bfloat16)
    return jnp.dot(hidden, down_proj, preferred_element_type=jnp.float32).astype(jnp.bfloat16)


def run_experts(received, gate_up, down_proj):
    flat = received.reshape(-1, received.shape[2])
    done = expert_rows(flat, gate_up, down_proj)
    return done.reshape(received.shape)


def moe_layer(current, layer_routes, gain_row, gate_up, down_proj, experts, capacity):
    tokens, features = current.shape
    widened = current.astype(jnp.float32)
    scale_inv = lax.rsqrt(jnp.mean(widened * widened, axis=-1, keepdims=True) + eps)
    normed = (widened * scale_inv * gain_row).astype(jnp.bfloat16)
    expert_ids = jnp.arange(experts, dtype=jnp.int32)
    onehot = (layer_routes[:, :, None] == expert_ids[None, None, :]).astype(jnp.int32)
    counted = jnp.sum(onehot, axis=1)
    before = jnp.cumsum(counted, axis=0) - counted
    slot_of = jnp.sum(onehot * (expert_ids[None, None, :] * capacity + before[:, None, :]), axis=2)
    slot_ids = jnp.arange(experts * capacity, dtype=jnp.int32)
    placing = jnp.sum(
        (slot_ids[:, None, None] == slot_of[None, :, :]).astype(jnp.int32), axis=2
    ).astype(jnp.bfloat16)
    outgoing = jnp.dot(placing, normed, preferred_element_type=jnp.float32).astype(jnp.bfloat16)
    outgoing = outgoing.reshape(experts, capacity, features)
    results = run_experts(
        lax.all_to_all(outgoing, "expert", split_axis=0, concat_axis=0, tiled=True),
        gate_up,
        down_proj,
    )
    returned = lax.all_to_all(results, "expert", split_axis=0, concat_axis=0, tiled=True).reshape(
        experts * capacity, features
    )
    combined = (
        jnp.einsum("it,id->td", placing, returned, preferred_element_type=jnp.float32) * 0.125
    )
    return (widened + combined).astype(jnp.bfloat16)


def on_device(inputs, routes, norm_gain, w_gate_up, w_down):
    experts = lax.axis_size("expert")
    sections = lax.axis_size("section")
    batches, tokens, features = inputs.shape
    top_k = routes.shape[3]
    capacity = min(tokens, 2 * tokens * top_k // experts)
    if sections == 1:
        layers_out = []
        previous = [inputs[batch_no] for batch_no in range(batches)]
        for layer_no in range(routes.shape[0]):
            current_layer = []
            for batch_no in range(batches):
                current_layer.append(
                    moe_layer(
                        previous[batch_no],
                        routes[layer_no, batch_no],
                        norm_gain[layer_no],
                        w_gate_up[layer_no, 0],
                        w_down[layer_no, 0],
                        experts,
                        capacity,
                    )
                )
            layers_out.append(jnp.stack(current_layer))
            previous = current_layer
        return jnp.stack(layers_out)
    segment_no = lax.axis_index("section")
    layer_routes = routes[0]
    gain_row = norm_gain[0]
    gate_up = w_gate_up[0, 0]
    down_proj = w_down[0, 0]
    handed = jnp.zeros((tokens, features), jnp.bfloat16)
    finished = []
    for turn_no in range(batches + 1):
        if turn_no < batches:
            fresh_rows = inputs[turn_no]
        else:
            fresh_rows = jnp.zeros((tokens, features), jnp.bfloat16)
        current = jnp.where(segment_no == 0, fresh_rows, handed)
        batch_pick = jnp.clip(turn_no - segment_no, 0, batches - 1)
        turn_routes = lax.dynamic_index_in_dim(layer_routes, batch_pick, 0, keepdims=False)
        result = moe_layer(current, turn_routes, gain_row, gate_up, down_proj, experts, capacity)
        finished.append(result)
        if turn_no < batches:
            handed = from_behind(result, "section", 1)
    first_segment = jnp.stack(finished[:batches])
    second_segment = jnp.stack(finished[1:])
    return jnp.where(segment_no == 0, first_segment, second_segment)[None]

LANES = 128
PAIR = 2
DEPTH = 4
TILE = 256
CHUNKS = 2
DOWN_PARTS = 2
KINDS = ("own", "z_in", "y_in", "y_out", "z_out", "done", "up", "down")
END_ORDER = (
    0, 4, 64, 8, 12, 41, 33, 34, 37, 35, 38, 39, 45, 42, 43, 66,
    69, 76, 67, 65, 70, 68, 192, 71, 47, 193, 73, 46, 194, 196, 197, 198,
    224, 74, 75, 72, 225, 228, 229, 78, 98, 99, 79, 77, 96, 200, 201, 202,
    204, 97, 101, 205, 206, 103, 232, 100, 102, 233, 130, 131, 236, 237, 129, 105,
    107, 106, 133, 104, 108, 135, 110, 134, 137, 109, 111, 160, 16, 138, 139, 164,
    20, 142, 143, 49, 53, 141, 81, 168, 24, 50, 51, 54, 85, 172, 28, 55,
    84, 57, 82, 83, 61, 80, 86, 87, 208, 209, 92, 59, 210, 88, 58, 212,
    213, 214, 93, 63, 89, 240, 241, 62, 91, 244, 114, 115, 90, 245, 216, 119,
    118, 94, 95, 117, 217, 116, 112, 218, 220, 221, 147, 222, 248, 249, 113, 151,
    146, 252, 121, 150, 253, 122, 123, 127, 149, 126, 145, 153, 125, 154, 155, 124,
    180, 159, 158, 120, 157, 184, 188, 176,
)
INNER_ORDER = (
    0, 8, 4, 12, 34, 33, 64, 41, 35, 37, 38, 39, 42, 66, 65, 43,
    67, 192, 73, 72, 47, 46, 45, 69, 70, 68, 193, 194, 71, 196, 197, 75,
    198, 74, 224, 225, 78, 228, 229, 77, 76, 200, 97, 103, 99, 102, 79, 201,
    101, 96, 202, 204, 205, 98, 206, 129, 232, 233, 236, 135, 237, 131, 105, 134,
    111, 110, 107, 106, 109, 108, 130, 104, 133, 100, 137, 143, 160, 16, 139, 138,
    50, 164, 20, 49, 142, 51, 82, 168, 54, 141, 53, 80, 24, 81, 84, 55,
    172, 28, 83, 58, 57, 88, 86, 85, 208, 87, 209, 59, 210, 212, 61, 213,
    62, 90, 63, 214, 240, 241, 244, 245, 113, 91, 93, 92, 89, 94, 95, 216,
    119, 115, 117, 217, 218, 220, 221, 222, 145, 118, 248, 249, 116, 252, 151, 147,
    123, 253, 122, 126, 125, 149, 121, 155, 127, 120, 158, 150, 154, 124, 157, 153,
    112, 114, 159, 146, 176, 184, 180, 188,
)


def flat_rows(block):
    return block.reshape(-1, block.shape[-1])


def unpack(code):
    code, number = divmod(code, 4)
    code, chunk = divmod(code, CHUNKS)
    code, batch = divmod(code, 2)
    kind, layer = divmod(code, 2)
    return KINDS[kind], layer, batch, chunk, number


def moe_kernel(
    count,
    x_hbm,
    routes_hbm,
    gain_hbm,
    gu_hbm,
    down_hbm,
    out_ref,
    x_ref,
    routes_ref,
    gain_ref,
    gu,
    down,
    rows,
    scaled,
    squares,
    joined,
    hidden,
    made,
    from_core,
    to_y,
    from_y,
    to_z,
    from_z,
    x_sem,
    w_sem,
    az_s,
    az_r,
    ap_s,
    ay_s,
    ay_r,
    ac_s,
    ac_r,
    rc_s,
    rc_r,
    ry_s,
    ry_r,
    rz_s,
    rz_r,
):
    layers, batches = routes_ref.shape[0], routes_ref.shape[1]
    tokens, features = x_ref.shape[1], x_ref.shape[2]
    units = down.shape[1]
    width = features // CHUNKS
    me = lax.axis_index("expert")
    c = lax.rem(me, PAIR)
    y = lax.rem(lax.div(me, PAIR), PAIR)
    z = lax.div(me, PAIR * PAIR)
    other_c, other_y = 1 - c, 1 - y

    def expert_at(zz, yy, cc):
        return (zz * PAIR + yy) * PAIR + cc

    low = z < DEPTH // 2
    inner = jnp.logical_and(z > 0, z < DEPTH - 1)

    def ranked(at_end, at_inner):
        upward = jnp.where(inner, at_inner, at_end)
        return jnp.where(low, upward, DEPTH - 1 - upward)

    near = [z, ranked(1, 2), ranked(2, 0), ranked(3, 3)]
    core_peer = expert_at(z, y, other_c)
    y_peer = expert_at(z, other_y, c)
    z_peers = [me] + [expert_at(near[n], y, c) for n in range(1, DEPTH)]

    def remote(src, dst, send, recv, target):
        return pltpu.make_async_remote_copy(
            src_ref=src,
            dst_ref=dst,
            send_sem=send,
            recv_sem=recv,
            device_id={"expert": target},
            device_id_type=pl.DeviceIdType.MESH,
        )

    barrier = pltpu.get_barrier_semaphore()
    for peer in z_peers[1:] + [core_peer, y_peer]:
        pl.semaphore_signal(
            barrier, inc=1, device_id={"expert": peer}, device_id_type=pl.DeviceIdType.MESH
        )

    inputs = ((x_hbm, x_ref), (routes_hbm, routes_ref), (gain_hbm, gain_ref))
    small = [
        pltpu.make_async_copy(source, target, x_sem.at[number])
        for number, (source, target) in enumerate(inputs)
    ]
    for load in small:
        load.start()
    for load in small:
        load.wait()
    loads = []
    for layer in range(layers):
        for number, (source, target) in enumerate(((gu_hbm, gu), (down_hbm, down))):
            load = pltpu.make_async_copy(
                source.at[layer, 0], target.at[layer], w_sem.at[layer, number]
            )
            load.start()
            loads.append(load)

    lanes = lax.broadcasted_iota(jnp.int32, (LANES, tokens), 0)
    named = jnp.zeros((LANES, tokens), jnp.float32)
    for lay in range(layers):
        for bat in range(batches):
            chosen = routes_ref[lay, bat] + (lay * batches + bat) * count
            for k in range(chosen.shape[0]):
                named = named + (chosen[k : k + 1, :] == lanes).astype(jnp.float32)
    same = lax.broadcasted_iota(jnp.int32, (tokens, tokens), 0) == lax.broadcasted_iota(
        jnp.int32, (tokens, tokens), 1
    )
    named = lax.dot_general(
        same.astype(jnp.bfloat16),
        named.astype(jnp.bfloat16),
        (((1,), (1,)), ((), ())),
        preferred_element_type=jnp.float32,
    )
    rows[0, c, y, z, :, pl.ds(features, LANES)] = named.astype(jnp.bfloat16)
    for bat in range(batches):
        rows[bat, c, y, z, :, pl.ds(0, features)] = x_ref[bat]
    pl.semaphore_wait(barrier, DEPTH + 1)

    def slot(layer, batch):
        return layer * batches + batch

    def cols(h):
        return pl.ds(h * width, width)

    def row_block(s, h, cc, yy, zz):
        extra = LANES if s == 0 and h == CHUNKS - 1 else 0
        return rows.at[s, cc, yy, zz, :, pl.ds(h * width, width + extra)]

    def gather_core(s, h, cc, yy, zz):
        block = row_block(s, h, cc, yy, zz)
        return remote(block, block, ac_s.at[s], ac_r.at[s, h, yy, zz], core_peer)

    def gather_y(s, h, yy, zz):
        block = row_block(s, h, c, yy, zz)
        return remote(block, block, ay_s.at[s], ay_r.at[s, h, zz], y_peer)

    def gather_z(s, h, n):
        block = row_block(s, h, c, y, z)
        return remote(block, block, az_s.at[s, n], az_r.at[s, h, z], z_peers[n])

    def gather_z_from(s, h, n):
        block = row_block(s, h, c, y, near[n])
        return remote(block, block, ap_s.at[s, n], az_r.at[s, h, near[n]], z_peers[2])

    def sum_core(s, h, cc, yy):
        return remote(
            made.at[s, cc, yy, :, :, cols(h)],
            from_core.at[s, yy, :, :, cols(h)],
            rc_s.at[s],
            rc_r.at[s, h, yy],
            core_peer,
        )

    def sum_y(s, h, zz):
        return remote(
            to_y.at[s, zz, :, cols(h)],
            from_y.at[s, zz, :, cols(h)],
            ry_s.at[s],
            ry_r.at[s, h, zz],
            y_peer,
        )

    def sum_z(s, h, n, source):
        return remote(
            to_z.at[s, near[n], :, cols(h)],
            from_z.at[s, source, :, cols(h)],
            rz_s.at[s],
            rz_r.at[s, h, source],
            z_peers[n],
        )

    def pair_sum(s, h, yy, zz):
        return made[s, c, yy, zz, :, cols(h)].astype(jnp.float32) + from_core[
            s, yy, zz, :, cols(h)
        ].astype(jnp.float32)

    class Place:
        def __init__(self, at_end):
            self.at_end = at_end
            self.seen = set()

        def once(self, build, *args, key):
            if (build, key) not in self.seen:
                self.seen.add((build, key))
                build(*args).wait_recv()

        def own(self, layer, batch, h, n):
            s = slot(layer, batch)
            gather_y(s, h, y, z).start()
            gather_z(s, h, 1).start()
            gather_z(s, h, 2).start()
            gather_core(s, h, c, y, z).start()

        def z_in(self, layer, batch, h, n):
            s = slot(layer, batch)
            gather_z_from(s, h, n).wait_recv()
            if not self.at_end and n != 2:
                gather_z_from(s, h, n).start()
            gather_y(s, h, y, near[n]).start()
            gather_core(s, h, c, y, near[n]).start()

        def y_in(self, layer, batch, h, n):
            s = slot(layer, batch)
            gather_y(s, h, other_y, near[n]).wait_recv()
            gather_core(s, h, c, other_y, near[n]).start()

        def y_out(self, layer, batch, h, n):
            s = slot(layer, batch)
            self.once(sum_core, s, h, other_c, other_y, key=(s, h, 1))
            to_y[s, near[n], :, cols(h)] = pair_sum(s, h, other_y, near[n]).astype(jnp.bfloat16)
            sum_y(s, h, near[n]).start()

        def z_out(self, layer, batch, h, n):
            s = slot(layer, batch)
            zz = near[n]
            self.once(sum_core, s, h, other_c, y, key=(s, h, 0))
            sum_y(s, h, zz).wait_recv()
            total = pair_sum(s, h, y, zz) + from_y[s, zz, :, cols(h)].astype(jnp.float32)
            to_z[s, zz, :, cols(h)] = total.astype(jnp.bfloat16)
            sum_z(s, h, n, z).start()

        def done(self, layer, batch, h, n):
            s = slot(layer, batch)
            self.once(sum_core, s, h, other_c, y, key=(s, h, 0))
            sum_y(s, h, z).wait_recv()
            total = pair_sum(s, h, y, z) + from_y[s, z, :, cols(h)].astype(jnp.float32)
            for r in range(1, DEPTH):
                sum_z(s, h, r, near[r]).wait_recv()
                total = total + from_z[s, near[r], :, cols(h)].astype(jnp.float32)
            source = x_ref if layer == 0 else out_ref.at[layer - 1]
            value = source[batch, :, cols(h)].astype(jnp.float32) + total * 0.125
            value = value.astype(jnp.bfloat16)
            out_ref[layer, batch, :, cols(h)] = value
            if layer + 1 < layers:
                rows[slot(layer + 1, batch), c, y, z, :, cols(h)] = value

    end, inside = Place(True), Place(False)

    def up(layer, batch, k, u):
        s = slot(layer, batch)
        if u == 0:
            for yy in (y, other_y):
                for n in range(DEPTH):
                    gather_core(s, k, other_c, yy, near[n]).wait_recv()
            if k == 0 and batch == 0:
                loads[2 * layer].wait()
            h = flat_rows(rows[s, :, :, :, :, cols(k)]).astype(jnp.float32)
            part = jnp.sum(h * h, axis=-1, keepdims=True)
            squares[...] = part if k == 0 else squares[...] + part
            scaled[...] = (h * gain_ref[pl.ds(layer, 1), cols(k)]).astype(jnp.bfloat16)
        x = scaled[...]
        mine_cols = (pl.ds(u * TILE, TILE), pl.ds(units + u * TILE, TILE))
        gate, lift = (
            jnp.dot(x, gu[layer, cols(k), where], preferred_element_type=jnp.float32)
            for where in mine_cols
        )
        if k > 0:
            gate, lift = joined[:, mine_cols[0]] + gate, joined[:, mine_cols[1]] + lift
        if k < CHUNKS - 1:
            joined[:, mine_cols[0]] = gate
            joined[:, mine_cols[1]] = lift
            return
        named = flat_rows(rows[0, :, :, :, :, pl.ds(features, LANES)]).astype(jnp.float32)
        lanes = lax.broadcasted_iota(jnp.int32, named.shape, 1)
        mine = jnp.sum(jnp.where(lanes == me + s * count, named, 0.0), axis=1, keepdims=True) > 0.5
        scale = lax.rsqrt(squares[...] * (1.0 / features) + eps)
        gate, lift = gate * scale, lift * scale
        value = gate / (1.0 + jnp.exp(-gate)) * lift
        hidden[:, pl.ds(u * TILE, TILE)] = jnp.where(mine, value, 0.0).astype(jnp.bfloat16)

    def down_part(layer, batch, h, u):
        s = slot(layer, batch)
        if h == 0 and u == 0 and batch == 0:
            loads[2 * layer + 1].wait()
        parts = DOWN_PARTS
        size = width // parts

        for j in range(size // TILE):
            where = pl.ds(h * width + u * size + j * TILE, TILE)
            result = jnp.dot(hidden[...], down[layer, :, where], preferred_element_type=jnp.float32)
            made[s, :, :, :, :, where] = result.astype(jnp.bfloat16).reshape(
                PAIR, PAIR, DEPTH, tokens, TILE
            )
        if u == parts - 1:
            sum_core(s, h, other_c, other_y).start()
            sum_core(s, h, other_c, y).start()

    def steps(place, codes):
        for code in codes:
            kind, *rest = unpack(code)
            getattr(place, kind)(*rest)

    def both(codes_end, codes_inside):
        if codes_end:
            pl.when(jnp.logical_not(inner))(functools.partial(steps, end, codes_end))
        if codes_inside:
            pl.when(inner)(functools.partial(steps, inside, codes_inside))

    def split(order):
        parts, heads = [[]], []
        for code in order:
            if unpack(code)[0] in ("up", "down"):
                heads.append(code)
                parts.append([])
            else:
                parts[-1].append(code)
        return parts, heads

    parts_end, heads = split(END_ORDER)
    parts_inside, _ = split(INNER_ORDER)
    both(parts_end[0], parts_inside[0])
    for code, codes_end, codes_inside in zip(heads, parts_end[1:], parts_inside[1:]):
        kind, *rest = unpack(code)
        (up if kind == "up" else down_part)(*rest)
        both(codes_end, codes_inside)
    def sent(block, sem):
        remote(block, block, sem, sem, core_peer).wait_send()

    for s in range(layers * batches):
        wide = pl.ds(0, features + (LANES if s == 0 else 0))
        sent(rows.at[s, c, :, :, :, wide], ac_s.at[s])
        sent(rows.at[s, c, y, :, :, wide], ay_s.at[s])
        sent(rows.at[s, c, y, z, :, wide], az_s.at[s, 1])
        sent(rows.at[s, c, y, z, :, wide], az_s.at[s, 2])
        sent(made.at[s, other_c], rc_s.at[s])
        sent(to_y.at[s], ry_s.at[s])
        sent(to_z.at[s, pl.ds(0, DEPTH - 1)], rz_s.at[s])

    @pl.when(inner)
    def _():
        for s in range(layers * batches):
            wide = pl.ds(0, features + (LANES if s == 0 else 0))
            sent(rows.at[s, c, y, z, :, wide], ap_s.at[s, 1])
            sent(rows.at[s, c, y, z, :, wide], ap_s.at[s, 3])


def fused_on_device(count, inputs, routes, norm_gain, w_gate_up, w_down):
    batches, tokens, features = inputs.shape
    layers = routes.shape[0]
    units = w_down.shape[2]
    slots = layers * batches
    bf16 = jnp.bfloat16
    vmem = pl.BlockSpec(memory_space=pltpu.VMEM)
    hbm = pl.BlockSpec(memory_space=pl.ANY)
    dma = pltpu.SemaphoreType.DMA
    by_z = pltpu.VMEM((slots, DEPTH, tokens, features), bf16)
    every = dma((slots, CHUNKS, DEPTH))
    return pl.pallas_call(
        functools.partial(moe_kernel, count),
        out_shape=pltpu.VMEM((layers, batches, tokens, features), bf16),
        in_specs=[hbm] * 5,
        out_specs=vmem,
        scratch_shapes=[
            pltpu.VMEM((batches, tokens, features), bf16),
            pltpu.VMEM((layers, batches, routes.shape[3], tokens), jnp.int32),
            pltpu.VMEM((layers, features), jnp.float32),
            pltpu.VMEM((layers, features, 2 * units), bf16),
            pltpu.VMEM((layers, units, features), bf16),
            pltpu.VMEM((slots, PAIR, PAIR, DEPTH, tokens, features + LANES), bf16),
            pltpu.VMEM((count * tokens, features // CHUNKS), bf16),
            pltpu.VMEM((count * tokens, 1), jnp.float32),
            pltpu.VMEM((count * tokens, 2 * units), jnp.float32),
            pltpu.VMEM((count * tokens, units), bf16),
            pltpu.VMEM((slots, PAIR, PAIR, DEPTH, tokens, features), bf16),
            pltpu.VMEM((slots, PAIR, DEPTH, tokens, features), bf16),
            by_z,
            by_z,
            by_z,
            by_z,
            dma((3,)),
            dma((layers, 2)),
            dma((slots, DEPTH)),
            every,
            dma((slots, DEPTH)),
            dma((slots,)),
            every,
            dma((slots,)),
            dma((slots, CHUNKS, PAIR, DEPTH)),
            dma((slots,)),
            dma((slots, CHUNKS, PAIR)),
            dma((slots,)),
            every,
            dma((slots,)),
            every,
        ],
        compiler_params=pltpu.CompilerParams(
            collective_id=0, has_side_effects=True, vmem_limit_bytes=58 << 20
        ),
        name="moe",
    )(inputs, jnp.swapaxes(routes, 2, 3), norm_gain, w_gate_up, w_down)


def choose(count, inputs, routes, norm_gain, w_gate_up, w_down):
    batches, tokens, features = inputs.shape
    layers = routes.shape[0]
    fits = layers == 2 and batches == 2 and layers * batches * count <= LANES
    tiled = w_down.shape[2] == 3 * TILE and features % (CHUNKS * DOWN_PARTS * TILE) == 0
    run = functools.partial(fused_on_device, count) if fits and tiled and tokens % 16 == 0 else on_device
    return run(inputs, routes, norm_gain, w_gate_up, w_down)


def solution(mesh):
    placed = (
        P(None, ("groups", "expert"), None),
        P("section", None, ("groups", "expert"), None),
        P("section", None),
        P("section", "expert", None, None),
        P("section", "expert", None, None),
    )
    count = mesh.shape["expert"]
    fused = mesh.shape["section"] == 1 and count == PAIR * PAIR * DEPTH
    return jax.shard_map(
        functools.partial(choose, count) if fused else on_device,
        mesh=mesh,
        in_specs=placed,
        out_specs=P("section", None, ("groups", "expert"), None),
        check_vma=False,
    )
```

```python
import functools

import jax
import jax.numpy as jnp
from jax import lax
from jax.experimental import pallas as pl
from jax.experimental.pallas import tpu as pltpu
from jax.sharding import PartitionSpec as P

eps = 1e-06


def from_behind(value, axis, steps):
    count = lax.axis_size(axis)
    initial, last = (max(0, -steps), min(count, count - steps))
    return lax.ppermute(value, axis, [(source, source + steps) for source in range(initial, last)])


def expert_rows(rows, gate_up, down_proj):
    hidden_size = down_proj.shape[0]
    joined = jnp.dot(rows, gate_up, preferred_element_type=jnp.float32)
    hidden = (jax.nn.silu(joined[:, :hidden_size]) * joined[:, hidden_size:]).astype(jnp.bfloat16)
    return jnp.dot(hidden, down_proj, preferred_element_type=jnp.float32).astype(jnp.bfloat16)


def run_experts(received, gate_up, down_proj):
    flat = received.reshape(-1, received.shape[2])
    done = expert_rows(flat, gate_up, down_proj)
    return done.reshape(received.shape)


def moe_layer(current, layer_routes, gain_row, gate_up, down_proj, experts, capacity):
    tokens, features = current.shape
    widened = current.astype(jnp.float32)
    scale_inv = lax.rsqrt(jnp.mean(widened * widened, axis=-1, keepdims=True) + eps)
    normed = (widened * scale_inv * gain_row).astype(jnp.bfloat16)
    expert_ids = jnp.arange(experts, dtype=jnp.int32)
    onehot = (layer_routes[:, :, None] == expert_ids[None, None, :]).astype(jnp.int32)
    counted = jnp.sum(onehot, axis=1)
    before = jnp.cumsum(counted, axis=0) - counted
    slot_of = jnp.sum(onehot * (expert_ids[None, None, :] * capacity + before[:, None, :]), axis=2)
    slot_ids = jnp.arange(experts * capacity, dtype=jnp.int32)
    placing = jnp.sum(
        (slot_ids[:, None, None] == slot_of[None, :, :]).astype(jnp.int32), axis=2
    ).astype(jnp.bfloat16)
    outgoing = jnp.dot(placing, normed, preferred_element_type=jnp.float32).astype(jnp.bfloat16)
    outgoing = outgoing.reshape(experts, capacity, features)
    results = run_experts(
        lax.all_to_all(outgoing, "expert", split_axis=0, concat_axis=0, tiled=True),
        gate_up,
        down_proj,
    )
    returned = lax.all_to_all(results, "expert", split_axis=0, concat_axis=0, tiled=True).reshape(
        experts * capacity, features
    )
    combined = (
        jnp.einsum("it,id->td", placing, returned, preferred_element_type=jnp.float32) * 0.125
    )
    return (widened + combined).astype(jnp.bfloat16)


def on_device(inputs, routes, norm_gain, w_gate_up, w_down):
    experts = lax.axis_size("expert")
    sections = lax.axis_size("section")
    batches, tokens, features = inputs.shape
    top_k = routes.shape[3]
    capacity = min(tokens, 2 * tokens * top_k // experts)
    if sections == 1:
        layers_out = []
        previous = [inputs[batch_no] for batch_no in range(batches)]
        for layer_no in range(routes.shape[0]):
            current_layer = []
            for batch_no in range(batches):
                current_layer.append(
                    moe_layer(
                        previous[batch_no],
                        routes[layer_no, batch_no],
                        norm_gain[layer_no],
                        w_gate_up[layer_no, 0],
                        w_down[layer_no, 0],
                        experts,
                        capacity,
                    )
                )
            layers_out.append(jnp.stack(current_layer))
            previous = current_layer
        return jnp.stack(layers_out)
    segment_no = lax.axis_index("section")
    layer_routes = routes[0]
    gain_row = norm_gain[0]
    gate_up = w_gate_up[0, 0]
    down_proj = w_down[0, 0]
    handed = jnp.zeros((tokens, features), jnp.bfloat16)
    finished = []
    for turn_no in range(batches + 1):
        if turn_no < batches:
            fresh_rows = inputs[turn_no]
        else:
            fresh_rows = jnp.zeros((tokens, features), jnp.bfloat16)
        current = jnp.where(segment_no == 0, fresh_rows, handed)
        batch_pick = jnp.clip(turn_no - segment_no, 0, batches - 1)
        turn_routes = lax.dynamic_index_in_dim(layer_routes, batch_pick, 0, keepdims=False)
        result = moe_layer(current, turn_routes, gain_row, gate_up, down_proj, experts, capacity)
        finished.append(result)
        if turn_no < batches:
            handed = from_behind(result, "section", 1)
    first_segment = jnp.stack(finished[:batches])
    second_segment = jnp.stack(finished[1:])
    return jnp.where(segment_no == 0, first_segment, second_segment)[None]

LANES = 128
PAIR = 2
DEPTH = 4
TILE = 256
CHUNKS = 2
DOWN_PARTS = 1
KINDS = ("own", "z_in", "y_in", "y_out", "z_out", "done", "up", "down")
ORDERS = (
    (
        (
            0, 8, 24, 16, 81, 128, 65, 136, 73, 152, 89, 144, 82, 129, 66, 67,
            153, 137, 74, 146, 90, 130, 75, 131, 384, 145, 385, 386, 91, 138, 154, 83,
            139, 392, 393, 394, 448, 155, 456, 388, 389, 147, 390, 396, 397, 195, 193, 194,
            398, 201, 203, 202, 200, 452, 460, 400, 401, 402, 408, 409, 410, 259, 192, 464,
            257, 472, 258, 404, 267, 405, 406, 266, 412, 413, 208, 209, 210, 211, 414, 216,
            265, 219, 218, 217, 468, 476, 320, 32, 273, 274, 328, 40, 275, 283, 97, 282,
            281, 160, 105, 168, 161, 98, 99, 169, 106, 336, 162, 48, 113, 344, 56, 107,
            163, 416, 417, 418, 170, 176, 114, 177, 184, 121, 171, 424, 425, 426, 480, 488,
            178, 420, 115, 421, 422, 122, 185, 123, 224, 226, 225, 227, 234, 235, 232, 233,
            428, 429, 430, 179, 484, 186, 492, 187, 432, 433, 434, 290, 440, 441, 289, 291,
            442, 496, 298, 504, 299, 241, 242, 240, 243, 297, 436, 437, 249, 250, 251, 248,
            438, 444, 445, 446, 500, 352, 508, 305, 306, 307, 313, 360, 314, 315, 368, 376,
        ),
        (
            8, 24, 0, 16, 89, 73, 65, 128, 144, 81, 90, 153, 152, 137, 136, 74,
            145, 75, 66, 154, 82, 91, 129, 138, 139, 67, 384, 130, 385, 386, 146, 83,
            155, 392, 131, 393, 394, 448, 456, 147, 388, 389, 390, 396, 397, 398, 452, 460,
            400, 401, 194, 193, 195, 402, 408, 201, 203, 192, 409, 410, 464, 472, 404, 405,
            406, 412, 413, 258, 414, 257, 468, 476, 259, 200, 202, 265, 208, 210, 209, 211,
            267, 219, 217, 266, 216, 320, 32, 274, 273, 97, 218, 328, 40, 275, 283, 281,
            282, 160, 161, 168, 98, 105, 416, 99, 417, 336, 162, 48, 418, 344, 56, 113,
            106, 169, 107, 424, 163, 176, 425, 114, 426, 121, 480, 488, 177, 420, 170, 421,
            422, 171, 428, 429, 430, 484, 178, 185, 122, 492, 184, 115, 123, 432, 433, 434,
            225, 226, 224, 227, 234, 235, 232, 233, 440, 441, 442, 496, 179, 504, 436, 437,
            438, 187, 186, 444, 289, 445, 290, 446, 500, 291, 299, 508, 298, 297, 241, 242,
            243, 240, 251, 250, 249, 248, 305, 306, 360, 352, 307, 315, 314, 313, 368, 376,
        ),
    ),
    (
        (
            16, 0, 8, 24, 66, 81, 144, 65, 136, 67, 74, 152, 73, 130, 128, 89,
            75, 129, 131, 384, 90, 385, 91, 82, 386, 138, 137, 83, 153, 139, 392, 145,
            393, 394, 448, 155, 154, 456, 146, 388, 389, 390, 396, 193, 195, 194, 192, 397,
            202, 203, 147, 200, 398, 201, 452, 460, 400, 401, 402, 408, 409, 257, 410, 464,
            259, 472, 258, 404, 266, 405, 406, 267, 412, 210, 208, 211, 209, 413, 216, 265,
            219, 218, 414, 468, 476, 217, 274, 275, 273, 320, 32, 283, 282, 328, 40, 281,
            97, 98, 160, 168, 99, 105, 161, 106, 336, 48, 162, 107, 163, 416, 417, 169,
            170, 418, 176, 113, 344, 56, 171, 424, 425, 426, 480, 114, 488, 420, 177, 421,
            122, 422, 115, 121, 184, 123, 224, 227, 225, 226, 232, 233, 234, 428, 178, 429,
            430, 186, 484, 179, 185, 492, 235, 432, 187, 433, 434, 440, 441, 291, 442, 289,
            496, 504, 290, 297, 242, 240, 243, 241, 298, 248, 250, 249, 251, 436, 437, 299,
            438, 444, 445, 446, 500, 508, 306, 352, 307, 305, 314, 313, 315, 360, 368, 376,
        ),
        (
            24, 8, 0, 16, 89, 152, 74, 136, 128, 73, 144, 75, 90, 65, 153, 81,
            138, 91, 66, 137, 67, 139, 82, 384, 385, 386, 154, 83, 129, 145, 130, 392,
            393, 131, 394, 448, 146, 456, 147, 388, 389, 390, 396, 397, 398, 452, 460, 400,
            401, 402, 408, 193, 194, 192, 195, 409, 201, 200, 155, 202, 203, 410, 464, 472,
            404, 405, 406, 412, 413, 414, 257, 468, 258, 476, 259, 265, 209, 210, 208, 211,
            266, 218, 219, 217, 267, 273, 216, 274, 320, 32, 275, 283, 282, 281, 160, 97,
            328, 40, 98, 416, 99, 417, 418, 161, 336, 48, 106, 105, 162, 107, 163, 168,
            424, 425, 113, 426, 344, 56, 176, 480, 170, 488, 169, 420, 171, 421, 422, 428,
            429, 114, 430, 177, 484, 121, 122, 492, 115, 123, 225, 226, 227, 432, 433, 233,
            178, 234, 184, 224, 232, 235, 434, 440, 441, 442, 496, 504, 185, 186, 179, 436,
            437, 438, 187, 444, 445, 446, 500, 289, 291, 290, 508, 297, 298, 243, 242, 299,
            240, 241, 250, 251, 249, 248, 307, 306, 352, 305, 314, 315, 313, 368, 376, 360,
        ),
    ),
)


def flat_rows(block):
    return block.reshape(-1, block.shape[-1])


def unpack(code):
    code, number = divmod(code, 8)
    code, chunk = divmod(code, CHUNKS)
    code, batch = divmod(code, 2)
    kind, layer = divmod(code, 2)
    return KINDS[kind], layer, batch, chunk, number


def moe_kernel(
    count,
    x_hbm,
    routes_hbm,
    gain_hbm,
    gu_hbm,
    down_hbm,
    out_ref,
    x_ref,
    routes_ref,
    gain_ref,
    gu,
    down,
    rows,
    scaled,
    squares,
    joined,
    hidden,
    made,
    from_core,
    to_y,
    from_y,
    to_z,
    from_z,
    x_sem,
    w_sem,
    az_s,
    az_r,
    ap_s,
    ay_s,
    ay_r,
    ac_s,
    ac_r,
    rc_s,
    rc_r,
    ry_s,
    ry_r,
    rz_s,
    rz_r,
):
    layers, batches = routes_ref.shape[0], routes_ref.shape[1]
    tokens, features = x_ref.shape[1], x_ref.shape[2]
    units = down.shape[1]
    width = features // CHUNKS
    me = lax.axis_index("expert")
    c = lax.rem(me, PAIR)
    y = lax.rem(lax.div(me, PAIR), PAIR)
    z = lax.div(me, PAIR * PAIR)
    other_c, other_y = 1 - c, 1 - y

    def expert_at(zz, yy, cc):
        return (zz * PAIR + yy) * PAIR + cc

    low = z < DEPTH // 2
    inner = jnp.logical_and(z > 0, z < DEPTH - 1)

    def ranked(at_end, at_inner):
        upward = jnp.where(inner, at_inner, at_end)
        return jnp.where(low, upward, DEPTH - 1 - upward)

    near = [z, ranked(1, 2), ranked(2, 0), ranked(3, 3)]
    core_peer = expert_at(z, y, other_c)
    y_peer = expert_at(z, other_y, c)
    z_peers = [me] + [expert_at(near[n], y, c) for n in range(1, DEPTH)]

    def remote(src, dst, send, recv, target):
        return pltpu.make_async_remote_copy(
            src_ref=src,
            dst_ref=dst,
            send_sem=send,
            recv_sem=recv,
            device_id={"expert": target},
            device_id_type=pl.DeviceIdType.MESH,
        )

    barrier = pltpu.get_barrier_semaphore()
    for peer in z_peers[1:] + [core_peer, y_peer]:
        pl.semaphore_signal(
            barrier, inc=1, device_id={"expert": peer}, device_id_type=pl.DeviceIdType.MESH
        )

    inputs = ((x_hbm, x_ref), (routes_hbm, routes_ref), (gain_hbm, gain_ref))
    small = [
        pltpu.make_async_copy(source, target, x_sem.at[number])
        for number, (source, target) in enumerate(inputs)
    ]
    for load in small:
        load.start()
    for load in small:
        load.wait()
    loads = []
    for layer in range(layers):
        for number, (source, target) in enumerate(((gu_hbm, gu), (down_hbm, down))):
            load = pltpu.make_async_copy(
                source.at[layer, 0], target.at[layer], w_sem.at[layer, number]
            )
            load.start()
            loads.append(load)

    lanes = lax.broadcasted_iota(jnp.int32, (LANES, tokens), 0)
    named = jnp.zeros((LANES, tokens), jnp.float32)
    for lay in range(layers):
        for bat in range(batches):
            chosen = routes_ref[lay, bat] + (lay * batches + bat) * count
            for k in range(chosen.shape[0]):
                named = named + (chosen[k : k + 1, :] == lanes).astype(jnp.float32)
    same = lax.broadcasted_iota(jnp.int32, (tokens, tokens), 0) == lax.broadcasted_iota(
        jnp.int32, (tokens, tokens), 1
    )
    named = lax.dot_general(
        same.astype(jnp.bfloat16),
        named.astype(jnp.bfloat16),
        (((1,), (1,)), ((), ())),
        preferred_element_type=jnp.float32,
    )
    rows[0, c, y, z, :, pl.ds(features, LANES)] = named.astype(jnp.bfloat16)
    for bat in range(batches):
        rows[bat, c, y, z, :, pl.ds(0, features)] = x_ref[bat]
    pl.semaphore_wait(barrier, DEPTH + 1)

    def slot(layer, batch):
        return layer * batches + batch

    def cols(h, s=None):
        return pl.ds(h * width, width + (LANES if s == 0 and h == CHUNKS - 1 else 0))

    def row_block(s, h, cc, yy, zz):
        return rows.at[s, cc, yy, zz, :, cols(h, s)]

    def gather_core(s, h, cc, yy, zz):
        block = row_block(s, h, cc, yy, zz)
        return remote(block, block, ac_s.at[s], ac_r.at[s, h], core_peer)

    def gather_y(s, h, yy, zz):
        block = row_block(s, h, c, yy, zz)
        return remote(block, block, ay_s.at[s], ay_r.at[s, h, zz], y_peer)

    def gather_z(s, h, n):
        block = row_block(s, h, c, y, z)
        return remote(block, block, az_s.at[s, n], az_r.at[s, h, z], z_peers[n])

    def gather_z_from(s, h, n):
        block = row_block(s, h, c, y, near[n])
        return remote(block, block, ap_s.at[s, n], az_r.at[s, h, near[n]], z_peers[2])

    def sum_core(s, h, cc, yy):
        return remote(
            made.at[s, cc, yy, :, :, cols(h)],
            from_core.at[s, yy, :, :, cols(h)],
            rc_s.at[s],
            rc_r.at[s, h, yy],
            core_peer,
        )

    def sum_y(s, h, zz):
        return remote(
            to_y.at[s, zz, :, cols(h)],
            from_y.at[s, zz, :, cols(h)],
            ry_s.at[s],
            ry_r.at[s, h, zz],
            y_peer,
        )

    def sum_z(s, h, n, source):
        return remote(
            to_z.at[s, near[n], :, cols(h)],
            from_z.at[s, source, :, cols(h)],
            rz_s.at[s],
            rz_r.at[s, h, source],
            z_peers[n],
        )

    def pair_sum(s, h, yy, zz):
        return made[s, c, yy, zz, :, cols(h)].astype(jnp.float32) + from_core[
            s, yy, zz, :, cols(h)
        ].astype(jnp.float32)

    class Place:
        def __init__(self, is_inner, core):
            self.at_end = not is_inner
            self.here = jnp.logical_and(inner if is_inner else jnp.logical_not(inner), c == core)
            self.steps = ORDERS[is_inner][core]
            self.seen = set()

        def once(self, build, *args, key):
            if (build, key) not in self.seen:
                self.seen.add((build, key))
                build(*args).wait_recv()

        def own(self, layer, batch, h, n):
            s = slot(layer, batch)
            gather_y(s, h, y, z).start()
            gather_z(s, h, 1).start()
            gather_z(s, h, 2).start()
            gather_core(s, h, c, y, z).start()

        def z_in(self, layer, batch, h, n):
            s = slot(layer, batch)
            gather_z_from(s, h, n).wait_recv()
            if not self.at_end and n != 2:
                gather_z_from(s, h, n).start()
            gather_y(s, h, y, near[n]).start()
            gather_core(s, h, c, y, near[n]).start()

        def y_in(self, layer, batch, h, n):
            s = slot(layer, batch)
            gather_y(s, h, other_y, near[n]).wait_recv()
            gather_core(s, h, c, other_y, near[n]).start()

        def y_out(self, layer, batch, h, n):
            s = slot(layer, batch)
            self.once(sum_core, s, h, other_c, other_y, key=(s, h, 1))
            to_y[s, near[n], :, cols(h)] = pair_sum(s, h, other_y, near[n]).astype(jnp.bfloat16)
            sum_y(s, h, near[n]).start()

        def z_out(self, layer, batch, h, n):
            s = slot(layer, batch)
            zz = near[n]
            self.once(sum_core, s, h, other_c, y, key=(s, h, 0))
            sum_y(s, h, zz).wait_recv()
            total = pair_sum(s, h, y, zz) + from_y[s, zz, :, cols(h)].astype(jnp.float32)
            to_z[s, zz, :, cols(h)] = total.astype(jnp.bfloat16)
            sum_z(s, h, n, z).start()

        def done(self, layer, batch, h, n):
            s = slot(layer, batch)
            self.once(sum_core, s, h, other_c, y, key=(s, h, 0))
            sum_y(s, h, z).wait_recv()
            total = pair_sum(s, h, y, z) + from_y[s, z, :, cols(h)].astype(jnp.float32)
            for r in range(1, DEPTH):
                sum_z(s, h, r, near[r]).wait_recv()
                total = total + from_z[s, near[r], :, cols(h)].astype(jnp.float32)
            source = x_ref if layer == 0 else out_ref.at[layer - 1]
            value = source[batch, :, cols(h)].astype(jnp.float32) + total * 0.125
            value = value.astype(jnp.bfloat16)
            out_ref[layer, batch, :, cols(h)] = value
            if layer + 1 < layers:
                rows[slot(layer + 1, batch), c, y, z, :, cols(h)] = value

    places = [Place(is_inner, core) for is_inner in (0, 1) for core in range(PAIR)]
    loaded = set()

    def weights(number):
        if number not in loaded:
            loaded.add(number)
            loads[number].wait()

    def up(layer, batch, k, number):
        s = slot(layer, batch)
        cc, u = divmod(number, 4)
        if u == 0:

            @pl.when(c != cc)
            def _():
                block = rows.at[s, other_c, :, :, :, cols(k, s)]
                remote(block, block, ac_s.at[s], ac_r.at[s, k], core_peer).wait_recv()

            weights(2 * layer)
            h = flat_rows(rows[s, cc, :, :, :, cols(k)]).astype(jnp.float32)
            part = jnp.sum(h * h, axis=-1, keepdims=True)
            squares[...] = part if k == 0 else squares[...] + part
            scaled[...] = (h * gain_ref[pl.ds(layer, 1), cols(k)]).astype(jnp.bfloat16)
        x = scaled[...]
        mine_cols = (pl.ds(u * TILE, TILE), pl.ds(units + u * TILE, TILE))
        gate, lift = (
            jnp.dot(x, gu[layer, cols(k), where], preferred_element_type=jnp.float32)
            for where in mine_cols
        )
        if k > 0:
            gate, lift = joined[:, mine_cols[0]] + gate, joined[:, mine_cols[1]] + lift
        if k < CHUNKS - 1:
            joined[:, mine_cols[0]] = gate
            joined[:, mine_cols[1]] = lift
            return
        named = flat_rows(rows[0, cc, :, :, :, pl.ds(features, LANES)]).astype(jnp.float32)
        lanes = lax.broadcasted_iota(jnp.int32, named.shape, 1)
        mine = jnp.sum(jnp.where(lanes == me + s * count, named, 0.0), axis=1, keepdims=True) > 0.5
        scale = lax.rsqrt(squares[...] * (1.0 / features) + eps)
        gate, lift = gate * scale, lift * scale
        value = gate / (1.0 + jnp.exp(-gate)) * lift
        hidden[:, pl.ds(u * TILE, TILE)] = jnp.where(mine, value, 0.0).astype(jnp.bfloat16)

    def down_part(layer, batch, h, number):
        s = slot(layer, batch)
        cc, u = divmod(number, 4)
        weights(2 * layer + 1)
        size = width // DOWN_PARTS
        for j in range(size // TILE):
            where = pl.ds(h * width + u * size + j * TILE, TILE)
            result = jnp.dot(hidden[...], down[layer, :, where], preferred_element_type=jnp.float32)
            made[s, cc, :, :, :, where] = result.astype(jnp.bfloat16).reshape(
                PAIR, DEPTH, tokens, TILE
            )
        if u == DOWN_PARTS - 1:

            @pl.when(c != cc)
            def _():
                sum_core(s, h, other_c, other_y).start()
                sum_core(s, h, other_c, y).start()

    def steps(place, codes):
        for code in codes:
            kind, *rest = unpack(code)
            getattr(place, kind)(*rest)

    def split(order):
        parts, heads = [[]], []
        for code in order:
            if unpack(code)[0] in ("up", "down"):
                heads.append(code)
                parts.append([])
            else:
                parts[-1].append(code)
        return parts, heads

    pieces = [split(place.steps) for place in places]
    for number, code in enumerate([None] + pieces[0][1]):
        if code is not None:
            kind, *rest = unpack(code)
            (up if kind == "up" else down_part)(*rest)
        for place, (parts, heads) in zip(places, pieces):
            if parts[number]:
                pl.when(place.here)(functools.partial(steps, place, parts[number]))

    def sent(block, sem):
        remote(block, block, sem, sem, core_peer).wait_send()

    for s in range(layers * batches):
        wide = pl.ds(0, features + (LANES if s == 0 else 0))
        sent(rows.at[s, c, :, :, :, wide], ac_s.at[s])
        sent(rows.at[s, c, y, :, :, wide], ay_s.at[s])
        sent(rows.at[s, c, y, z, :, wide], az_s.at[s, 1])
        sent(rows.at[s, c, y, z, :, wide], az_s.at[s, 2])
        sent(made.at[s, other_c], rc_s.at[s])
        sent(to_y.at[s], ry_s.at[s])
        sent(to_z.at[s, pl.ds(0, DEPTH - 1)], rz_s.at[s])

    @pl.when(inner)
    def _():
        for s in range(layers * batches):
            wide = pl.ds(0, features + (LANES if s == 0 else 0))
            sent(rows.at[s, c, y, z, :, wide], ap_s.at[s, 1])
            sent(rows.at[s, c, y, z, :, wide], ap_s.at[s, 3])


def fused_on_device(count, inputs, routes, norm_gain, w_gate_up, w_down):
    batches, tokens, features = inputs.shape
    layers = routes.shape[0]
    units = w_down.shape[2]
    slots = layers * batches
    half = count * tokens // PAIR
    bf16 = jnp.bfloat16
    vmem = pl.BlockSpec(memory_space=pltpu.VMEM)
    hbm = pl.BlockSpec(memory_space=pl.ANY)
    dma = pltpu.SemaphoreType.DMA
    by_z = pltpu.VMEM((slots, DEPTH, tokens, features), bf16)
    every = dma((slots, CHUNKS, DEPTH))
    return pl.pallas_call(
        functools.partial(moe_kernel, count),
        out_shape=pltpu.VMEM((layers, batches, tokens, features), bf16),
        in_specs=[hbm] * 5,
        out_specs=vmem,
        scratch_shapes=[
            pltpu.VMEM((batches, tokens, features), bf16),
            pltpu.VMEM((layers, batches, routes.shape[3], tokens), jnp.int32),
            pltpu.VMEM((layers, features), jnp.float32),
            pltpu.VMEM((layers, features, 2 * units), bf16),
            pltpu.VMEM((layers, units, features), bf16),
            pltpu.VMEM((slots, PAIR, PAIR, DEPTH, tokens, features + LANES), bf16),
            pltpu.VMEM((half, features // CHUNKS), bf16),
            pltpu.VMEM((half, 1), jnp.float32),
            pltpu.VMEM((half, 2 * units), jnp.float32),
            pltpu.VMEM((half, units), bf16),
            pltpu.VMEM((slots, PAIR, PAIR, DEPTH, tokens, features), bf16),
            pltpu.VMEM((slots, PAIR, DEPTH, tokens, features), bf16),
            by_z,
            by_z,
            by_z,
            by_z,
            dma((3,)),
            dma((layers, 2)),
            dma((slots, DEPTH)),
            every,
            dma((slots, DEPTH)),
            dma((slots,)),
            every,
            dma((slots,)),
            dma((slots, CHUNKS)),
            dma((slots,)),
            dma((slots, CHUNKS, PAIR)),
            dma((slots,)),
            every,
            dma((slots,)),
            every,
        ],
        compiler_params=pltpu.CompilerParams(
            collective_id=0, has_side_effects=True, vmem_limit_bytes=58 << 20
        ),
        name="moe",
    )(inputs, jnp.swapaxes(routes, 2, 3), norm_gain, w_gate_up, w_down)


def choose(count, inputs, routes, norm_gain, w_gate_up, w_down):
    batches, tokens, features = inputs.shape
    layers = routes.shape[0]
    fits = layers == 2 and batches == 2 and layers * batches * count <= LANES
    tiled = w_down.shape[2] == 3 * TILE and features % (CHUNKS * DOWN_PARTS * TILE) == 0
    run = functools.partial(fused_on_device, count) if fits and tiled and tokens % 16 == 0 else on_device
    return run(inputs, routes, norm_gain, w_gate_up, w_down)


def solution(mesh):
    placed = (
        P(None, ("groups", "expert"), None),
        P("section", None, ("groups", "expert"), None),
        P("section", None),
        P("section", "expert", None, None),
        P("section", "expert", None, None),
    )
    count = mesh.shape["expert"]
    fused = mesh.shape["section"] == 1 and count == PAIR * PAIR * DEPTH
    return jax.shard_map(
        functools.partial(choose, count) if fused else on_device,
        mesh=mesh,
        in_specs=placed,
        out_specs=P("section", None, ("groups", "expert"), None),
        check_vma=False,
    )
```

```python
import functools

import jax
import jax.numpy as jnp
from jax import lax
from jax.experimental import pallas as pl
from jax.experimental.pallas import tpu as pltpu
from jax.sharding import PartitionSpec as P

eps = 1e-06


def from_behind(value, axis, steps):
    count = lax.axis_size(axis)
    initial, last = (max(0, -steps), min(count, count - steps))
    return lax.ppermute(value, axis, [(source, source + steps) for source in range(initial, last)])


def expert_rows(rows, gate_up, down_proj):
    hidden_size = down_proj.shape[0]
    joined = jnp.dot(rows, gate_up, preferred_element_type=jnp.float32)
    hidden = (jax.nn.silu(joined[:, :hidden_size]) * joined[:, hidden_size:]).astype(jnp.bfloat16)
    return jnp.dot(hidden, down_proj, preferred_element_type=jnp.float32).astype(jnp.bfloat16)


def run_experts(received, gate_up, down_proj):
    flat = received.reshape(-1, received.shape[2])
    done = expert_rows(flat, gate_up, down_proj)
    return done.reshape(received.shape)


def moe_layer(current, layer_routes, gain_row, gate_up, down_proj, experts, capacity):
    tokens, features = current.shape
    widened = current.astype(jnp.float32)
    scale_inv = lax.rsqrt(jnp.mean(widened * widened, axis=-1, keepdims=True) + eps)
    normed = (widened * scale_inv * gain_row).astype(jnp.bfloat16)
    expert_ids = jnp.arange(experts, dtype=jnp.int32)
    onehot = (layer_routes[:, :, None] == expert_ids[None, None, :]).astype(jnp.int32)
    counted = jnp.sum(onehot, axis=1)
    before = jnp.cumsum(counted, axis=0) - counted
    slot_of = jnp.sum(onehot * (expert_ids[None, None, :] * capacity + before[:, None, :]), axis=2)
    slot_ids = jnp.arange(experts * capacity, dtype=jnp.int32)
    placing = jnp.sum(
        (slot_ids[:, None, None] == slot_of[None, :, :]).astype(jnp.int32), axis=2
    ).astype(jnp.bfloat16)
    outgoing = jnp.dot(placing, normed, preferred_element_type=jnp.float32).astype(jnp.bfloat16)
    outgoing = outgoing.reshape(experts, capacity, features)
    results = run_experts(
        lax.all_to_all(outgoing, "expert", split_axis=0, concat_axis=0, tiled=True),
        gate_up,
        down_proj,
    )
    returned = lax.all_to_all(results, "expert", split_axis=0, concat_axis=0, tiled=True).reshape(
        experts * capacity, features
    )
    combined = (
        jnp.einsum("it,id->td", placing, returned, preferred_element_type=jnp.float32) * 0.125
    )
    return (widened + combined).astype(jnp.bfloat16)


def on_device(inputs, routes, norm_gain, w_gate_up, w_down):
    experts = lax.axis_size("expert")
    sections = lax.axis_size("section")
    batches, tokens, features = inputs.shape
    top_k = routes.shape[3]
    capacity = min(tokens, 2 * tokens * top_k // experts)
    if sections == 1:
        layers_out = []
        previous = [inputs[batch_no] for batch_no in range(batches)]
        for layer_no in range(routes.shape[0]):
            current_layer = []
            for batch_no in range(batches):
                current_layer.append(
                    moe_layer(
                        previous[batch_no],
                        routes[layer_no, batch_no],
                        norm_gain[layer_no],
                        w_gate_up[layer_no, 0],
                        w_down[layer_no, 0],
                        experts,
                        capacity,
                    )
                )
            layers_out.append(jnp.stack(current_layer))
            previous = current_layer
        return jnp.stack(layers_out)
    segment_no = lax.axis_index("section")
    layer_routes = routes[0]
    gain_row = norm_gain[0]
    gate_up = w_gate_up[0, 0]
    down_proj = w_down[0, 0]
    handed = jnp.zeros((tokens, features), jnp.bfloat16)
    finished = []
    for turn_no in range(batches + 1):
        if turn_no < batches:
            fresh_rows = inputs[turn_no]
        else:
            fresh_rows = jnp.zeros((tokens, features), jnp.bfloat16)
        current = jnp.where(segment_no == 0, fresh_rows, handed)
        batch_pick = jnp.clip(turn_no - segment_no, 0, batches - 1)
        turn_routes = lax.dynamic_index_in_dim(layer_routes, batch_pick, 0, keepdims=False)
        result = moe_layer(current, turn_routes, gain_row, gate_up, down_proj, experts, capacity)
        finished.append(result)
        if turn_no < batches:
            handed = from_behind(result, "section", 1)
    first_segment = jnp.stack(finished[:batches])
    second_segment = jnp.stack(finished[1:])
    return jnp.where(segment_no == 0, first_segment, second_segment)[None]

LANES = 128
PAIR = 2
DEPTH = 4
TILE = 256
CHUNKS = 2
DOWN_PARTS = 1
KINDS = ("own", "z_in", "y_in", "y_out", "z_out", "done", "up", "down")
ORDERS = (
    (
        (
            0, 8, 24, 16, 81, 128, 65, 136, 73, 152, 89, 144, 82, 129, 66, 67,
            153, 137, 74, 146, 90, 130, 75, 131, 384, 145, 385, 386, 91, 138, 154, 83,
            139, 392, 393, 394, 448, 155, 456, 388, 389, 147, 390, 396, 397, 195, 193, 194,
            398, 201, 203, 202, 200, 452, 460, 400, 401, 402, 408, 409, 410, 259, 192, 464,
            257, 472, 258, 404, 267, 405, 406, 266, 412, 413, 208, 209, 210, 211, 414, 216,
            265, 219, 218, 217, 468, 476, 320, 32, 273, 274, 328, 40, 275, 283, 97, 282,
            281, 160, 105, 168, 161, 98, 99, 169, 106, 336, 162, 48, 113, 344, 56, 107,
            163, 416, 417, 418, 170, 176, 114, 177, 184, 121, 171, 424, 425, 426, 480, 488,
            178, 420, 115, 421, 422, 122, 185, 123, 224, 226, 225, 227, 234, 235, 232, 233,
            428, 429, 430, 179, 484, 186, 492, 187, 432, 433, 434, 290, 440, 441, 289, 291,
            442, 496, 298, 504, 299, 241, 242, 240, 243, 297, 436, 437, 249, 250, 251, 248,
            438, 444, 445, 446, 500, 352, 508, 305, 306, 307, 313, 360, 314, 315, 368, 376,
        ),
        (
            8, 24, 0, 16, 89, 73, 65, 128, 144, 81, 90, 153, 152, 137, 136, 74,
            145, 75, 66, 154, 82, 91, 129, 138, 139, 67, 384, 130, 385, 386, 146, 83,
            155, 392, 131, 393, 394, 448, 456, 147, 388, 389, 390, 396, 397, 398, 452, 460,
            400, 401, 194, 193, 195, 402, 408, 201, 203, 192, 409, 410, 464, 472, 404, 405,
            406, 412, 413, 258, 414, 257, 468, 476, 259, 200, 202, 265, 208, 210, 209, 211,
            267, 219, 217, 266, 216, 320, 32, 274, 273, 97, 218, 328, 40, 275, 283, 281,
            282, 160, 161, 168, 98, 105, 416, 99, 417, 336, 162, 48, 418, 344, 56, 113,
            106, 169, 107, 424, 163, 176, 425, 114, 426, 121, 480, 488, 177, 420, 170, 421,
            422, 171, 428, 429, 430, 484, 178, 185, 122, 492, 184, 115, 123, 432, 433, 434,
            225, 226, 224, 227, 234, 235, 232, 233, 440, 441, 442, 496, 179, 504, 436, 437,
            438, 187, 186, 444, 289, 445, 290, 446, 500, 291, 299, 508, 298, 297, 241, 242,
            243, 240, 251, 250, 249, 248, 305, 306, 360, 352, 307, 315, 314, 313, 368, 376,
        ),
    ),
    (
        (
            16, 0, 8, 24, 66, 81, 144, 65, 136, 67, 74, 152, 73, 130, 128, 89,
            75, 129, 131, 384, 90, 385, 91, 82, 386, 138, 137, 83, 153, 139, 392, 145,
            393, 394, 448, 155, 154, 456, 146, 388, 389, 390, 396, 193, 195, 194, 192, 397,
            202, 203, 147, 200, 398, 201, 452, 460, 400, 401, 402, 408, 409, 257, 410, 464,
            259, 472, 258, 404, 266, 405, 406, 267, 412, 210, 208, 211, 209, 413, 216, 265,
            219, 218, 414, 468, 476, 217, 274, 275, 273, 320, 32, 283, 282, 328, 40, 281,
            97, 98, 160, 168, 99, 105, 161, 106, 336, 48, 162, 107, 163, 416, 417, 169,
            170, 418, 176, 113, 344, 56, 171, 424, 425, 426, 480, 114, 488, 420, 177, 421,
            122, 422, 115, 121, 184, 123, 224, 227, 225, 226, 232, 233, 234, 428, 178, 429,
            430, 186, 484, 179, 185, 492, 235, 432, 187, 433, 434, 440, 441, 291, 442, 289,
            496, 504, 290, 297, 242, 240, 243, 241, 298, 248, 250, 249, 251, 436, 437, 299,
            438, 444, 445, 446, 500, 508, 306, 352, 307, 305, 314, 313, 315, 360, 368, 376,
        ),
        (
            24, 8, 0, 16, 89, 152, 74, 136, 128, 73, 144, 75, 90, 65, 153, 81,
            138, 91, 66, 137, 67, 139, 82, 384, 385, 386, 154, 83, 129, 145, 130, 392,
            393, 131, 394, 448, 146, 456, 147, 388, 389, 390, 396, 397, 398, 452, 460, 400,
            401, 402, 408, 193, 194, 192, 195, 409, 201, 200, 155, 202, 203, 410, 464, 472,
            404, 405, 406, 412, 413, 414, 257, 468, 258, 476, 259, 265, 209, 210, 208, 211,
            266, 218, 219, 217, 267, 273, 216, 274, 320, 32, 275, 283, 282, 281, 160, 97,
            328, 40, 98, 416, 99, 417, 418, 161, 336, 48, 106, 105, 162, 107, 163, 168,
            424, 425, 113, 426, 344, 56, 176, 480, 170, 488, 169, 420, 171, 421, 422, 428,
            429, 114, 430, 177, 484, 121, 122, 492, 115, 123, 225, 226, 227, 432, 433, 233,
            178, 234, 184, 224, 232, 235, 434, 440, 441, 442, 496, 504, 185, 186, 179, 436,
            437, 438, 187, 444, 445, 446, 500, 289, 291, 290, 508, 297, 298, 243, 242, 299,
            240, 241, 250, 251, 249, 248, 307, 306, 352, 305, 314, 315, 313, 368, 376, 360,
        ),
    ),
)


def flat_rows(block):
    return block.reshape(-1, block.shape[-1])


def unpack(code):
    code, number = divmod(code, 8)
    code, chunk = divmod(code, CHUNKS)
    code, batch = divmod(code, 2)
    kind, layer = divmod(code, 2)
    return KINDS[kind], layer, batch, chunk, number


def moe_kernel(
    count,
    x_hbm,
    routes_hbm,
    gain_hbm,
    gu_hbm,
    down_hbm,
    out_ref,
    x_ref,
    routes_ref,
    gain_ref,
    gu,
    down,
    rows,
    scaled,
    squares,
    joined,
    hidden,
    made,
    from_core,
    to_y,
    from_y,
    to_z,
    from_z,
    x_sem,
    w_sem,
    az_s,
    az_r,
    ap_s,
    ay_s,
    ay_r,
    ac_s,
    ac_r,
    rc_s,
    rc_r,
    ry_s,
    ry_r,
    rz_s,
    rz_r,
):
    layers, batches = routes_ref.shape[0], routes_ref.shape[1]
    tokens, features = x_ref.shape[1], x_ref.shape[2]
    units = down.shape[1]
    width = features // CHUNKS
    me = lax.axis_index("expert")
    c = lax.rem(me, PAIR)
    y = lax.rem(lax.div(me, PAIR), PAIR)
    z = lax.div(me, PAIR * PAIR)
    other_c, other_y = 1 - c, 1 - y

    def expert_at(zz, yy, cc):
        return (zz * PAIR + yy) * PAIR + cc

    low = z < DEPTH // 2
    inner = jnp.logical_and(z > 0, z < DEPTH - 1)

    def ranked(at_end, at_inner):
        upward = jnp.where(inner, at_inner, at_end)
        return jnp.where(low, upward, DEPTH - 1 - upward)

    near = [z, ranked(1, 2), ranked(2, 0), ranked(3, 3)]
    core_peer = expert_at(z, y, other_c)
    y_peer = expert_at(z, other_y, c)
    z_peers = [me] + [expert_at(near[n], y, c) for n in range(1, DEPTH)]

    def remote(src, dst, send, recv, target):
        return pltpu.make_async_remote_copy(
            src_ref=src,
            dst_ref=dst,
            send_sem=send,
            recv_sem=recv,
            device_id={"expert": target},
            device_id_type=pl.DeviceIdType.MESH,
        )

    barrier = pltpu.get_barrier_semaphore()
    for peer in z_peers[1:] + [core_peer, y_peer]:
        pl.semaphore_signal(
            barrier, inc=1, device_id={"expert": peer}, device_id_type=pl.DeviceIdType.MESH
        )

    inputs = ((x_hbm, x_ref), (routes_hbm, routes_ref), (gain_hbm, gain_ref))
    small = [
        pltpu.make_async_copy(source, target, x_sem.at[number])
        for number, (source, target) in enumerate(inputs)
    ]
    for load in small:
        load.start()
    for load in small:
        load.wait()
    loads = []
    for layer in range(layers):
        for number, (source, target) in enumerate(((gu_hbm, gu), (down_hbm, down))):
            load = pltpu.make_async_copy(
                source.at[layer, 0], target.at[layer], w_sem.at[layer, number]
            )
            load.start()
            loads.append(load)

    lanes = lax.broadcasted_iota(jnp.int32, (LANES, tokens), 0)
    named = jnp.zeros((LANES, tokens), jnp.float32)
    for lay in range(layers):
        for bat in range(batches):
            chosen = routes_ref[lay, bat] + (lay * batches + bat) * count
            for k in range(chosen.shape[0]):
                named = named + (chosen[k : k + 1, :] == lanes).astype(jnp.float32)
    same = lax.broadcasted_iota(jnp.int32, (tokens, tokens), 0) == lax.broadcasted_iota(
        jnp.int32, (tokens, tokens), 1
    )
    named = lax.dot_general(
        same.astype(jnp.bfloat16),
        named.astype(jnp.bfloat16),
        (((1,), (1,)), ((), ())),
        preferred_element_type=jnp.float32,
    )
    rows[0, c, y, z, :, pl.ds(features, LANES)] = named.astype(jnp.bfloat16)
    for bat in range(batches):
        rows[bat, c, y, z, :, pl.ds(0, features)] = x_ref[bat]
    pl.semaphore_wait(barrier, DEPTH + 1)

    def slot(layer, batch):
        return layer * batches + batch

    def cols(h, s=None):
        return pl.ds(h * width, width + (LANES if s == 0 and h == CHUNKS - 1 else 0))

    def row_block(s, h, cc, yy, zz):
        return rows.at[s, cc, yy, zz, :, cols(h, s)]

    def gather_core(s, h, cc, yy, zz):
        block = row_block(s, h, cc, yy, zz)
        return remote(block, block, ac_s.at[s], ac_r.at[s, h], core_peer)

    def gather_y(s, h, yy, zz):
        block = row_block(s, h, c, yy, zz)
        return remote(block, block, ay_s.at[s], ay_r.at[s % PAIR, h, zz], y_peer)

    def gather_z(s, h, n):
        block = row_block(s, h, c, y, z)
        return remote(block, block, az_s.at[s, n], az_r.at[s % PAIR, h, z], z_peers[n])

    def gather_z_from(s, h, n):
        block = row_block(s, h, c, y, near[n])
        return remote(block, block, ap_s.at[s, n], az_r.at[s % PAIR, h, near[n]], z_peers[2])

    def sum_core(s, h, cc, yy):
        return remote(
            made.at[s, cc, yy, :, :, cols(h)],
            from_core.at[s, yy, :, :, cols(h)],
            rc_s.at[s],
            rc_r.at[s % PAIR, h, yy],
            core_peer,
        )

    def sum_y(s, h, zz):
        return remote(
            to_y.at[s, zz, :, cols(h)],
            from_y.at[s, zz, :, cols(h)],
            ry_s.at[s],
            ry_r.at[s % PAIR, h, zz],
            y_peer,
        )

    def sum_z(s, h, n, source):
        return remote(
            to_z.at[s, near[n], :, cols(h)],
            from_z.at[s, source, :, cols(h)],
            rz_s.at[s],
            rz_r.at[s % PAIR, h, source],
            z_peers[n],
        )

    def pair_sum(s, h, yy, zz):
        return made[s, c, yy, zz, :, cols(h)].astype(jnp.float32) + from_core[
            s, yy, zz, :, cols(h)
        ].astype(jnp.float32)

    class Place:
        def __init__(self, is_inner, core):
            self.at_end = not is_inner
            self.here = jnp.logical_and(inner if is_inner else jnp.logical_not(inner), c == core)
            self.steps = ORDERS[is_inner][core]
            self.seen = set()

        def once(self, build, *args, key):
            if (build, key) not in self.seen:
                self.seen.add((build, key))
                build(*args).wait_recv()

        def own(self, layer, batch, h, n):
            s = slot(layer, batch)
            gather_y(s, h, y, z).start()
            gather_z(s, h, 1).start()
            gather_z(s, h, 2).start()
            gather_core(s, h, c, y, z).start()

        def z_in(self, layer, batch, h, n):
            s = slot(layer, batch)
            gather_z_from(s, h, n).wait_recv()
            if not self.at_end and n != 2:
                gather_z_from(s, h, n).start()
            gather_y(s, h, y, near[n]).start()
            gather_core(s, h, c, y, near[n]).start()

        def y_in(self, layer, batch, h, n):
            s = slot(layer, batch)
            gather_y(s, h, other_y, near[n]).wait_recv()
            gather_core(s, h, c, other_y, near[n]).start()

        def y_out(self, layer, batch, h, n):
            s = slot(layer, batch)
            self.once(sum_core, s, h, other_c, other_y, key=(s, h, 1))
            to_y[s, near[n], :, cols(h)] = pair_sum(s, h, other_y, near[n]).astype(jnp.bfloat16)
            sum_y(s, h, near[n]).start()

        def z_out(self, layer, batch, h, n):
            s = slot(layer, batch)
            zz = near[n]
            self.once(sum_core, s, h, other_c, y, key=(s, h, 0))
            sum_y(s, h, zz).wait_recv()
            total = pair_sum(s, h, y, zz) + from_y[s, zz, :, cols(h)].astype(jnp.float32)
            to_z[s, zz, :, cols(h)] = total.astype(jnp.bfloat16)
            sum_z(s, h, n, z).start()

        def done(self, layer, batch, h, n):
            s = slot(layer, batch)
            self.once(sum_core, s, h, other_c, y, key=(s, h, 0))
            sum_y(s, h, z).wait_recv()
            total = pair_sum(s, h, y, z) + from_y[s, z, :, cols(h)].astype(jnp.float32)
            for r in range(1, DEPTH):
                sum_z(s, h, r, near[r]).wait_recv()
                total = total + from_z[s, near[r], :, cols(h)].astype(jnp.float32)
            source = x_ref if layer == 0 else out_ref.at[layer - 1]
            value = source[batch, :, cols(h)].astype(jnp.float32) + total * 0.125
            value = value.astype(jnp.bfloat16)
            out_ref[layer, batch, :, cols(h)] = value
            if layer + 1 < layers:
                rows[slot(layer + 1, batch), c, y, z, :, cols(h)] = value

    places = [Place(is_inner, core) for is_inner in (0, 1) for core in range(PAIR)]
    loaded = set()

    def weights(number):
        if number not in loaded:
            loaded.add(number)
            loads[number].wait()

    def up(layer, batch, k, number):
        s = slot(layer, batch)
        cc, u = divmod(number, 4)
        if u == 0:

            @pl.when(c != cc)
            def _():
                block = rows.at[s, other_c, :, :, :, cols(k, s)]
                remote(block, block, ac_s.at[s], ac_r.at[s, k], core_peer).wait_recv()

            weights(2 * layer)
            h = flat_rows(rows[s, cc, :, :, :, cols(k)]).astype(jnp.float32)
            part = jnp.sum(h * h, axis=-1, keepdims=True)
            squares[...] = part if k == 0 else squares[...] + part
            scaled[...] = (h * gain_ref[pl.ds(layer, 1), cols(k)]).astype(jnp.bfloat16)
        x = scaled[...]
        mine_cols = (pl.ds(u * TILE, TILE), pl.ds(units + u * TILE, TILE))
        gate, lift = (
            jnp.dot(x, gu[layer, cols(k), where], preferred_element_type=jnp.float32)
            for where in mine_cols
        )
        if k > 0:
            gate, lift = joined[:, mine_cols[0]] + gate, joined[:, mine_cols[1]] + lift
        if k < CHUNKS - 1:
            joined[:, mine_cols[0]] = gate
            joined[:, mine_cols[1]] = lift
            return
        named = flat_rows(rows[0, cc, :, :, :, pl.ds(features, LANES)]).astype(jnp.float32)
        lanes = lax.broadcasted_iota(jnp.int32, named.shape, 1)
        mine = jnp.sum(jnp.where(lanes == me + s * count, named, 0.0), axis=1, keepdims=True) > 0.5
        scale = lax.rsqrt(squares[...] * (1.0 / features) + eps)
        gate, lift = gate * scale, lift * scale
        value = gate / (1.0 + jnp.exp(-gate)) * lift
        hidden[:, pl.ds(u * TILE, TILE)] = jnp.where(mine, value, 0.0).astype(jnp.bfloat16)

    def down_part(layer, batch, h, number):
        s = slot(layer, batch)
        cc, u = divmod(number, 4)
        weights(2 * layer + 1)
        size = width // DOWN_PARTS
        for j in range(size // TILE):
            where = pl.ds(h * width + u * size + j * TILE, TILE)
            result = jnp.dot(hidden[...], down[layer, :, where], preferred_element_type=jnp.float32)
            made[s, cc, :, :, :, where] = result.astype(jnp.bfloat16).reshape(
                PAIR, DEPTH, tokens, TILE
            )
        if u == DOWN_PARTS - 1:

            @pl.when(c != cc)
            def _():
                sum_core(s, h, other_c, other_y).start()
                sum_core(s, h, other_c, y).start()

    def steps(place, codes):
        for code in codes:
            kind, *rest = unpack(code)
            getattr(place, kind)(*rest)

    def split(order):
        parts, heads = [[]], []
        for code in order:
            if unpack(code)[0] in ("up", "down"):
                heads.append(code)
                parts.append([])
            else:
                parts[-1].append(code)
        return parts, heads

    pieces = [split(place.steps) for place in places]
    for number, code in enumerate([None] + pieces[0][1]):
        if code is not None:
            kind, *rest = unpack(code)
            (up if kind == "up" else down_part)(*rest)
        for place, (parts, heads) in zip(places, pieces):
            if parts[number]:
                pl.when(place.here)(functools.partial(steps, place, parts[number]))

    def sent(block, sem):
        remote(block, block, sem, sem, core_peer).wait_send()

    for s in range(layers * batches):
        wide = pl.ds(0, features + (LANES if s == 0 else 0))
        sent(rows.at[s, c, :, :, :, wide], ac_s.at[s])
        sent(rows.at[s, c, y, :, :, wide], ay_s.at[s])
        sent(rows.at[s, c, y, z, :, wide], az_s.at[s, 1])
        sent(rows.at[s, c, y, z, :, wide], az_s.at[s, 2])
        sent(made.at[s, other_c], rc_s.at[s])
        sent(to_y.at[s], ry_s.at[s])
        sent(to_z.at[s, pl.ds(0, DEPTH - 1)], rz_s.at[s])

    @pl.when(inner)
    def _():
        for s in range(layers * batches):
            wide = pl.ds(0, features + (LANES if s == 0 else 0))
            sent(rows.at[s, c, y, z, :, wide], ap_s.at[s, 1])
            sent(rows.at[s, c, y, z, :, wide], ap_s.at[s, 3])


def fused_on_device(count, inputs, routes, norm_gain, w_gate_up, w_down):
    batches, tokens, features = inputs.shape
    layers = routes.shape[0]
    units = w_down.shape[2]
    slots = layers * batches
    half = count * tokens // PAIR
    bf16 = jnp.bfloat16
    vmem = pl.BlockSpec(memory_space=pltpu.VMEM)
    hbm = pl.BlockSpec(memory_space=pl.ANY)
    dma = pltpu.SemaphoreType.DMA
    by_z = pltpu.VMEM((slots, DEPTH, tokens, features), bf16)
    every = dma((batches, CHUNKS, DEPTH))
    return pl.pallas_call(
        functools.partial(moe_kernel, count),
        out_shape=pltpu.VMEM((layers, batches, tokens, features), bf16),
        in_specs=[hbm] * 5,
        out_specs=vmem,
        scratch_shapes=[
            pltpu.VMEM((batches, tokens, features), bf16),
            pltpu.VMEM((layers, batches, routes.shape[3], tokens), jnp.int32),
            pltpu.VMEM((layers, features), jnp.float32),
            pltpu.VMEM((layers, features, 2 * units), bf16),
            pltpu.VMEM((layers, units, features), bf16),
            pltpu.VMEM((slots, PAIR, PAIR, DEPTH, tokens, features + LANES), bf16),
            pltpu.VMEM((half, features // CHUNKS), bf16),
            pltpu.VMEM((half, 1), jnp.float32),
            pltpu.VMEM((half, 2 * units), jnp.float32),
            pltpu.VMEM((half, units), bf16),
            pltpu.VMEM((slots, PAIR, PAIR, DEPTH, tokens, features), bf16),
            pltpu.VMEM((slots, PAIR, DEPTH, tokens, features), bf16),
            by_z,
            by_z,
            by_z,
            by_z,
            dma((3,)),
            dma((layers, 2)),
            dma((slots, DEPTH)),
            every,
            dma((slots, DEPTH)),
            dma((slots,)),
            every,
            dma((slots,)),
            dma((slots, CHUNKS)),
            dma((slots,)),
            dma((batches, CHUNKS, PAIR)),
            dma((slots,)),
            every,
            dma((slots,)),
            every,
        ],
        compiler_params=pltpu.CompilerParams(
            collective_id=0, has_side_effects=True, vmem_limit_bytes=58 << 20
        ),
        name="moe",
    )(inputs, jnp.swapaxes(routes, 2, 3), norm_gain, w_gate_up, w_down)


def choose(count, inputs, routes, norm_gain, w_gate_up, w_down):
    batches, tokens, features = inputs.shape
    layers = routes.shape[0]
    fits = layers == 2 and batches == 2 and layers * batches * count <= LANES
    tiled = w_down.shape[2] == 3 * TILE and features % (CHUNKS * DOWN_PARTS * TILE) == 0
    run = functools.partial(fused_on_device, count) if fits and tiled and tokens % 16 == 0 else on_device
    return run(inputs, routes, norm_gain, w_gate_up, w_down)


def solution(mesh):
    placed = (
        P(None, ("groups", "expert"), None),
        P("section", None, ("groups", "expert"), None),
        P("section", None),
        P("section", "expert", None, None),
        P("section", "expert", None, None),
    )
    count = mesh.shape["expert"]
    fused = mesh.shape["section"] == 1 and count == PAIR * PAIR * DEPTH
    return jax.shard_map(
        functools.partial(choose, count) if fused else on_device,
        mesh=mesh,
        in_specs=placed,
        out_specs=P("section", None, ("groups", "expert"), None),
        check_vma=False,
    )
```
